32 devices in a mesh: groups: 2 (over y), section: 4 (over x, core), lat: 4 (over z).
Axes of the slice: x: 2, y: 2, z: 4, core: 2. Of those that a mesh axis runs over, the one named last changes fastest.
Arguments:
- member_slabs: float32 [8, 16, 64, 768], P(('groups', 'section'), 'lat'), parts along dimension 0, may hold values from -6 to 6
- member_codes: int32 [2, 8], P(None, 'groups'), parts along dimension 1, may hold values from 0 to 31
- member_table: float32 [32, 768], replicated, may hold values from -4 to 4
- land_sea: int32 [16, 64], P('lat'), may hold values 0 or 1
- land_embed: float32 [4, 768], P('section'), may hold values from -4 to 4
- attention_gain: float32 [4, 768], P('section'), may hold values from 0.25 to 1.75
- project_in: bfloat16 [4, 768, 2304], P('section'), may hold values from -0.21875 to 0.21875
- logit_scale: float32 [4, 12], P('section'), may hold values from 3 to 25
- position_kernel: float32 [4, 5, 3, 768], P('section'), may hold values from -1.5 to 1.5
- project_out: bfloat16 [4, 768, 768], P('section'), may hold values from -0.21875 to 0.21875
- feed_gain: float32 [4, 768], P('section'), may hold values from 0.25 to 1.75
- expand_weight: bfloat16 [4, 768, 2048], P('section'), may hold values from -0.21875 to 0.21875
- reduce_weight: bfloat16 [4, 2048, 768], P('section'), may hold values from -0.125 to 0.125
- window_offset: int32 [4], P('section'), may hold values from 1 to 31
Outputs:
- updated_slabs: float32 [8, 16, 64, 768], P(('groups', 'section'), 'lat'), parts along dimension 0
The draws below stay inside these ranges and needn't reach their ends.
There are 2 independent parts, one for each index of `groups`. The reference program is written for one: setup_inputs(seed, part) draws one part's arguments, and reference() takes and returns one part's arrays. A program takes and returns all parts, laid end to end along the dimension named above; an argument that names none is the same for every part. Nothing has to cross between parts.
Inputs may be any that keep to these rules, and one draw needn't show every extreme that they name: member_codes[t, m] names the perturbation embedding of member m at tick t. `land_sea`: 1 marks land.
All inputs are finite; a program needn't handle non-finite values. No bound on the sum of `land_sea` on one device may be relied on, other than what follows from the above.
Results may differ from the reference program's by a relative error of at most 0.0085.
Values may be sent and summed in bfloat16 or wider, within the bound.
A program may use at most 128 MiB of HBM per device.

```python
import math
import jax
import jax.numpy as jnp
from jax import lax

D = 768
HEADS = 12
FF = 2048
WIN_LAT = 4
WIN_LON = 32
LONS = 64
TICKS = 2
TABLE = 32
LATS = 16
LAYERS = 4
MEMBERS = 4
N_SECTION = 4


def with_ends(result, rng, smallest, top_value):
    longest = result.shape.index(max(result.shape))
    spots = []
    for shift in (0, 1):
        where = [jax.random.randint(jax.random.fold_in(rng, axis), (), 0, length) for axis, length in enumerate(result.shape)]
        where[longest] = (where[longest] + shift) % result.shape[longest]
        spots.append(tuple(where))
    return result.at[spots[0]].set(smallest).at[spots[1]].set(top_value)


def levels(key, shape, cuts, least, largest):
    factor_of, own = 1.0, jax.random.fold_in(key, 6)
    for dim, parts in cuts:
        draws = jnp.exp(jax.random.uniform(jax.random.fold_in(own, dim), (parts,), jnp.float32, least / len(cuts), largest / len(cuts)))
        factor_of = factor_of * jnp.repeat(draws, shape[dim] // parts).reshape([-1 if axis == dim else 1 for axis in range(len(shape))])
    return factor_of


def normal_values(key, extent, spread, limit, cuts=(), kind=jnp.bfloat16):
    loudness = levels(key, extent, cuts, -0.22, 0.18) if cuts else 1.0
    entries = jax.random.normal(key, extent, jnp.float32) * spread * loudness
    return jnp.minimum(jnp.maximum(entries, -limit), limit).astype(kind)


def setup_inputs(seed: int = 0, part: int = 0) -> dict:
    key_list = jax.random.split(jax.random.key(seed), 15)
    part_splits = jax.random.split(jax.random.fold_in(key_list[14], part), 15)
    member_slabs = normal_values(part_splits[0], (MEMBERS, LATS, LONS, D), 1.0, 6.0, ((0, 4), (1, 4)), jnp.float32)
    member_codes = with_ends(jax.random.randint(part_splits[1], (TICKS, MEMBERS), 0, TABLE), jax.random.fold_in(part_splits[1], 1), 0, TABLE - 1).astype(jnp.int32)
    member_table = normal_values(key_list[2], (TABLE, D), 0.5, 4.0, (), jnp.float32)
    land_sea = with_ends((jax.random.randint(key_list[3], (LATS, LONS), 0, 10) < 3).astype(jnp.int32), jax.random.fold_in(key_list[3], 1), 0, 1)
    land_embed = normal_values(key_list[4], (LAYERS, D), 0.5, 4.0, ((0, 4),), jnp.float32)
    attention_gain = jnp.clip(1.0 + 0.15 * jax.random.normal(key_list[5], (LAYERS, D), jnp.float32), 0.25, 1.75)
    project_in = normal_values(key_list[6], (LAYERS, D, 3 * D), D ** -0.5, 0.21875, ((0, 4),))
    logit_scale = jnp.clip(jnp.exp(math.log(25.0) - 2.1202635 * jax.random.uniform(key_list[7], (LAYERS, HEADS), jnp.float32) ** levels(key_list[7], (LAYERS, HEADS), ((0, 4),), -0.2, 0.2)), 3.0, 25.0)
    position_kernel = normal_values(key_list[8], (LAYERS, WIN_LAT + 1, 3, D), (3 * (WIN_LAT + 1)) ** -0.5, 1.5, ((0, 4),), jnp.float32)
    project_out = normal_values(key_list[9], (LAYERS, D, D), D ** -0.5, 0.21875, ((0, 4),))
    feed_gain = jnp.clip(1.0 + 0.15 * jax.random.normal(key_list[10], (LAYERS, D), jnp.float32), 0.25, 1.75)
    expand_weight = normal_values(key_list[11], (LAYERS, D, FF), D ** -0.5, 0.21875, ((0, 4),))
    reduce_weight = normal_values(key_list[12], (LAYERS, FF, D), FF ** -0.5, 0.125, ((0, 4),))
    window_offset = with_ends(jax.random.randint(key_list[13], (LAYERS,), 1, WIN_LON), jax.random.fold_in(key_list[13], 1), 1, WIN_LON - 1).astype(jnp.int32)
    return {"member_slabs": member_slabs, "member_codes": member_codes, "member_table": member_table, "land_sea": land_sea, "land_embed": land_embed, "attention_gain": attention_gain, "project_in": project_in, "logit_scale": logit_scale, "position_kernel": position_kernel, "project_out": project_out, "feed_gain": feed_gain, "expand_weight": expand_weight, "reduce_weight": reduce_weight, "window_offset": window_offset}


EPSILON = 1e-06

def norm_scale(values, gain_row):
    mean_square = lax.optimization_barrier(jnp.mean(values * values, axis=-1, keepdims=True))
    return values * lax.rsqrt(mean_square + EPSILON) * gain_row

def head_unit(values):
    shaped = values.reshape(values.shape[:-1] + (HEADS, values.shape[-1] // HEADS))
    square_sum = lax.optimization_barrier(jnp.sum(shaped * shaped, axis=-1, keepdims=True))
    return (shaped * lax.rsqrt(square_sum + EPSILON)).astype(jnp.bfloat16)

def position_term(value_rows, kernel, band_rows):
    totals = jnp.zeros((band_rows,) + value_rows.shape[1:], jnp.float32)
    for lat_step in range(kernel.shape[0]):
        strip_rows = value_rows[lat_step:lat_step + band_rows]
        for lon_step in range(kernel.shape[1]):
            totals = totals + kernel[lat_step, lon_step] * jnp.roll(strip_rows, 1 - lon_step, axis=1)
    return totals

def window_attend(query_tiles, key_tiles, value_tiles, row_valid, head_scale):
    row_count, lon_count, head_count, head_width = query_tiles.shape
    tile_rows = row_count // WIN_LAT
    tile_cols = lon_count // WIN_LON

    def to_tiles(block_in):
        shaped = block_in.reshape(tile_rows, WIN_LAT, tile_cols, WIN_LON, head_count, head_width)
        shaped = shaped.transpose(0, 2, 4, 1, 3, 5)
        return shaped.reshape(tile_rows, tile_cols, head_count, WIN_LAT * WIN_LON, head_width)
    query_set = to_tiles(query_tiles).astype(jnp.float32)
    key_set = to_tiles(key_tiles).astype(jnp.float32)
    value_set = to_tiles(value_tiles).astype(jnp.float32)
    scores = jnp.einsum('abhqd,abhkd->abhqk', query_set, key_set) * head_scale.reshape(1, 1, head_count, 1, 1)
    key_keep = jnp.broadcast_to(row_valid.reshape(tile_rows, 1, 1, 1, WIN_LAT, 1), (tile_rows, 1, 1, 1, WIN_LAT, WIN_LON))
    key_keep = key_keep.reshape(tile_rows, 1, 1, 1, WIN_LAT * WIN_LON).astype(jnp.float32)
    raised = jnp.exp(scores) * key_keep
    weights = (raised / lax.optimization_barrier(jnp.sum(raised, axis=-1, keepdims=True))).astype(jnp.bfloat16)
    weights = lax.optimization_barrier(weights).astype(jnp.float32)
    attended = jnp.einsum('abhqk,abhkd->abhqd', weights, value_set)
    regrid = attended.reshape(tile_rows, tile_cols, head_count, WIN_LAT, WIN_LON, head_width).transpose(0, 3, 1, 4, 2, 5)
    return regrid.reshape(row_count, lon_count, head_count * head_width)

def apply_layer(current, perturb, land_sea, layer_index, land_embed, attention_gain, project_in, logit_scale, position_kernel, project_out, feed_gain, expand_weight, reduce_weight, window_offset):
    band_rows, lon_cells, features = current.shape
    halo_rows = WIN_LAT // 2
    head_width = features // HEADS
    stream = current + perturb + land_sea.astype(jnp.float32)[:, :, None] * land_embed[layer_index]
    normed = norm_scale(stream, attention_gain[layer_index]).astype(jnp.bfloat16).reshape(-1, features)
    queries = jnp.dot(normed, project_in[layer_index][:, :features], preferred_element_type=jnp.float32)
    key_value = jnp.dot(normed, project_in[layer_index][:, features:], preferred_element_type=jnp.float32)
    query_unit = head_unit(queries).reshape(band_rows, lon_cells, HEADS, head_width)
    key_unit = head_unit(key_value[:, :features]).reshape(band_rows, lon_cells, HEADS, head_width)
    value_half = key_value[:, features:].astype(jnp.bfloat16).reshape(band_rows, lon_cells, features)
    value_float = lax.optimization_barrier(value_half).astype(jnp.float32)
    value_padded = jnp.pad(value_float, ((halo_rows, halo_rows), (0, 0), (0, 0)))
    position = position_term(value_padded, position_kernel[layer_index], band_rows)
    value_heads = value_half.reshape(band_rows, lon_cells, HEADS, head_width)
    if layer_index % 2 == 1:
        offset = window_offset[layer_index]
        row_pad = ((halo_rows, halo_rows), (0, 0), (0, 0), (0, 0))

        def prepare(block_in):
            return jnp.roll(jnp.pad(block_in, row_pad), -offset, axis=1)
        row_valid = jnp.pad(jnp.ones((band_rows,), bool), (halo_rows, halo_rows))
        attended = window_attend(prepare(query_unit), prepare(key_unit), prepare(value_heads), row_valid, logit_scale[layer_index])
        attended = jnp.roll(attended, offset, axis=1)[halo_rows:halo_rows + band_rows]
    else:
        attended = window_attend(query_unit, key_unit, value_heads, jnp.ones((band_rows,), bool), logit_scale[layer_index])
    blended = (attended + position).astype(jnp.bfloat16).reshape(-1, features)
    after_mix = stream + jnp.dot(blended, project_out[layer_index], preferred_element_type=jnp.float32).reshape(stream.shape)
    normed_mix = norm_scale(after_mix, feed_gain[layer_index]).astype(jnp.bfloat16).reshape(-1, features)
    hidden = jax.nn.gelu(jnp.dot(normed_mix, expand_weight[layer_index], preferred_element_type=jnp.float32), approximate=False).astype(jnp.bfloat16)
    return after_mix + jnp.dot(hidden, reduce_weight[layer_index], preferred_element_type=jnp.float32).reshape(stream.shape)

def reference(member_slabs, member_codes, member_table, land_sea, land_embed, attention_gain, project_in, logit_scale, position_kernel, project_out, feed_gain, expand_weight, reduce_weight, window_offset):
    current = member_slabs
    for tick_index in range(TICKS):
        updated = []
        for section_index in range(N_SECTION):
            member = (section_index - tick_index) % N_SECTION
            perturb = member_table[member_codes[tick_index, member]]
            updated.append(apply_layer(current[section_index], perturb, land_sea, section_index, land_embed, attention_gain, project_in, logit_scale, position_kernel, project_out, feed_gain, expand_weight, reduce_weight, window_offset))
        current = jnp.stack(updated)
        if tick_index + 1 < TICKS:
            current = jnp.roll(current, 1, axis=0)
    return current
```

```python
import contextlib
import functools
import math

import jax
import jax.numpy as jnp
from jax import lax
from jax.experimental import pallas as pl
from jax.experimental.pallas import tpu as pltpu
from jax.sharding import PartitionSpec as P

WIN_LAT = 4
WIN_LON = 32
TICKS = 2
EPSILON = 1e-06

F32 = jnp.float32
BF16 = jnp.bfloat16
LANES = 128
COLS = 256
ROWS = 32
AHEAD = 1
MESH = pl.DeviceIdType.MESH


def mark(name):
    return contextlib.nullcontext()


def norm_scale(values, gain_row):
    mean_square = jnp.mean(values * values, axis=-1, keepdims=True)
    return values * lax.rsqrt(mean_square + EPSILON) * gain_row


def dot(left, right):
    return jnp.dot(left, right, preferred_element_type=F32)


def head_unit(values, head_width):
    groups = []
    for start in range(0, values.shape[1], LANES):
        part = values[:, start : start + LANES]
        lane = lax.broadcasted_iota(jnp.int32, part.shape, 1)
        square = part * part
        factor = None
        for low in range(0, LANES, head_width):
            inside = (lane >= low) & (lane < low + head_width)
            total = jnp.sum(jnp.where(inside, square, 0.0), axis=-1, keepdims=True)
            scale = lax.rsqrt(total + EPSILON)
            factor = scale if factor is None else jnp.where(inside, scale, factor)
        groups.append((part * factor).astype(BF16))
    return jnp.concatenate(groups, axis=1)


def kernel(
    sizes,
    codes_hbm,
    offsets_hbm,
    scale_hbm,
    slab_hbm,
    table_hbm,
    land_hbm,
    embed_hbm,
    attention_gain_hbm,
    feed_gain_hbm,
    taps_hbm,
    in_hbm,
    out_hbm,
    up_hbm,
    down_hbm,
    result,
    codes,
    offsets,
    head_scale,
    slab,
    table,
    land,
    land_embed,
    attention_gain,
    feed_gain,
    position_kernel,
    w_in,
    w_out,
    w_up,
    w_down,
    stream,
    mixed,
    normed_here,
    normed,
    halo,
    queries,
    keys,
    values,
    attended,
    position,
    rolled,
    blended,
    normed_mix,
    hidden,
    order,
    land_column,
    ring_out,
    ring_in,
    load_sem,
    halo_send,
    halo_recv,
    ring_send,
    ring_recv,
):
    section_count, band_count, head_width = sizes
    pieces, band_rows, span, features = slab.shape
    lon_cells = pieces * span
    chunk = band_rows * span
    half = chunk // 2
    tokens = pieces * chunk
    per_group = LANES // head_width
    parts = features // COLS
    section = lax.axis_index("section")
    band = lax.axis_index("lat")
    following = lax.rem(section + 1, section_count)
    preceding = lax.rem(section + section_count - 1, section_count)
    has_low = band > 0
    has_high = band < band_count - 1
    shifted = lax.rem(section, 2)
    odd = shifted == 1
    even = shifted == 0

    barrier = pltpu.get_barrier_semaphore()
    pl.semaphore_signal(barrier, inc=1, device_id={"section": following}, device_id_type=MESH)
    pl.semaphore_signal(barrier, inc=1, device_id={"section": preceding}, device_id_type=MESH)

    @pl.when(has_low)
    def _():
        pl.semaphore_signal(barrier, inc=1, device_id={"lat": band - 1}, device_id_type=MESH)

    @pl.when(has_high)
    def _():
        pl.semaphore_signal(barrier, inc=1, device_id={"lat": band + 1}, device_id_type=MESH)

    pairs = [
        (slab_hbm.at[:, pl.ds(piece * span, span), :], slab.at[piece]) for piece in range(pieces)
    ]
    pairs += [
        (codes_hbm, codes),
        (offsets_hbm, offsets),
        (scale_hbm, head_scale),
        (table_hbm, table),
        (land_hbm, land),
        (embed_hbm, land_embed),
        (attention_gain_hbm, attention_gain),
        (feed_gain_hbm, feed_gain),
        (taps_hbm, position_kernel),
    ]
    small = len(pairs)
    for start in range(0, features, COLS):
        for base in range(0, 3 * features, features):
            columns = pl.ds(base + start, COLS)
            pairs.append((in_hbm.at[:, columns], w_in.at[:, columns]))
    wide = len(pairs)
    pairs += [(out_hbm, w_out), (up_hbm, w_up), (down_hbm, w_down)]
    loads = [
        pltpu.make_async_copy(source, target, load_sem.at[index])
        for index, (source, target) in enumerate(pairs)
    ]
    for load in loads:
        load.start()

    @pl.when(jnp.logical_not(has_low))
    def _():
        halo[:, 0] = jnp.zeros(halo.shape[:1] + halo.shape[2:], BF16)

    @pl.when(jnp.logical_not(has_high))
    def _():
        halo[:, 1] = jnp.zeros(halo.shape[:1] + halo.shape[2:], BF16)

    with mark("small"):
        for load in loads[:small]:
            load.wait()

    offset = offsets[0, 0]
    square = (lon_cells, lon_cells)
    diagonal = lax.broadcasted_iota(jnp.int32, square, 0) == lax.broadcasted_iota(jnp.int32, square, 1)
    for row in range(band_rows):
        marks = jnp.broadcast_to(land[row : row + 1, :].astype(F32), square)
        column = jnp.sum(jnp.where(diagonal, marks, 0.0), axis=-1, keepdims=True)
        for piece in range(pieces):
            first = piece * chunk + row * span
            land_column[first : first + span, :] = column[piece * span : (piece + 1) * span]

    def fill_order():
        for way, turn in enumerate((offset, lon_cells - offset)):
            for piece in range(pieces):
                for row in range(band_rows):
                    lon = lax.broadcasted_iota(jnp.int32, (span, tokens), 0) + piece * span + turn
                    lon = jnp.where(lon >= lon_cells, lon - lon_cells, lon)
                    target = lon + row * span
                    for step in range(1, pieces):
                        target = target + jnp.where(lon >= step * span, chunk - span, 0)
                    source = lax.broadcasted_iota(jnp.int32, (span, tokens), 1)
                    first = piece * chunk + row * span
                    order[way, first : first + span, :] = jnp.where(target == source, 1.0, 0.0).astype(BF16)

    lane = lax.broadcasted_iota(jnp.int32, (1, LANES), 1)
    own = [
        jnp.where((lane >= low) & (lane < low + head_width), 1.0, 0.0).astype(BF16)
        for low in range(0, LANES, head_width)
    ]
    key_lane = lax.broadcasted_iota(jnp.int32, (1, chunk), 1)
    keeps = [
        jnp.where((key_lane >= half) | has_low, 1.0, 0.0),
        jnp.where((key_lane < half) | has_high, 1.0, 0.0),
    ]

    def halo_up(tick, piece):
        return pltpu.make_async_remote_copy(
            src_ref=normed.at[tick, piece, pl.ds(half, half)],
            dst_ref=halo.at[tick, 0, piece],
            send_sem=halo_send.at[tick, piece, 0],
            recv_sem=halo_recv.at[tick, piece, 0],
            device_id={"lat": jnp.minimum(band + 1, band_count - 1)},
            device_id_type=MESH,
        )

    def halo_down(tick, piece):
        return pltpu.make_async_remote_copy(
            src_ref=normed.at[tick, piece, pl.ds(0, half)],
            dst_ref=halo.at[tick, 1, piece],
            send_sem=halo_send.at[tick, piece, 1],
            recv_sem=halo_recv.at[tick, piece, 1],
            device_id={"lat": jnp.maximum(band - 1, 0)},
            device_id_type=MESH,
        )

    def start_halo(tick, which):
        @pl.when(has_high)
        def _():
            for piece in which:
                halo_up(tick, piece).start()

        @pl.when(has_low)
        def _():
            for piece in which:
                halo_down(tick, piece).start()

    def wait_halo(tick):
        @pl.when(has_high)
        def _():
            for piece in range(pieces):
                halo_down(tick, piece).wait_recv()

        @pl.when(has_low)
        def _():
            for piece in range(pieces):
                halo_up(tick, piece).wait_recv()

    def drain_halo(tick):
        @pl.when(has_high)
        def _():
            for piece in range(pieces):
                halo_up(tick, piece).wait_send()

        @pl.when(has_low)
        def _():
            for piece in range(pieces):
                halo_down(tick, piece).wait_send()

    def ring_copy(tick, piece):
        return pltpu.make_async_remote_copy(
            src_ref=ring_out.at[tick, piece],
            dst_ref=ring_in.at[tick, piece],
            send_sem=ring_send.at[tick, piece],
            recv_sem=ring_recv.at[tick, piece],
            device_id={"section": following},
            device_id_type=MESH,
        )

    def wait_barrier():
        ends = (band == 0).astype(jnp.int32) + (band == band_count - 1).astype(jnp.int32)
        pl.semaphore_wait(barrier, 4 - ends)

    def enter(tick, piece, perturb, target):
        for row in range(band_rows):
            first = row * span
            rows = slice(piece * chunk + first, piece * chunk + first + span)
            if tick == 0:
                current = slab[piece, row]
            else:
                current = ring_in[tick - 1, piece, first : first + span, :].astype(F32)
            current = current + perturb + land_column[rows, :] * land_embed[...]
            stream[rows, :] = current
            target[piece, first : first + span, :] = norm_scale(current, attention_gain[...]).astype(BF16)

    def roll_rows(way, source, store):
        for part in range(parts):
            columns = slice(part * COLS, (part + 1) * COLS)
            for piece in range(pieces):
                moved = dot(order[way, piece * chunk : (piece + 1) * chunk, :], source(columns))
                store(piece, columns, moved.astype(BF16))

    def project_own(tick, piece):
        rows = normed[tick, piece]
        for part in range(parts):
            start = part * COLS
            columns = slice(start, start + COLS)
            queries[piece, :, columns] = head_unit(dot(rows, w_in[:, columns]), head_width)
            keys[piece, half : half + chunk, columns] = head_unit(
                dot(rows, w_in[:, features + start : features + start + COLS]), head_width
            )
            values[piece, half : half + chunk, columns] = dot(
                rows, w_in[:, 2 * features + start : 2 * features + start + COLS]
            ).astype(BF16)

    def project_halo(tick, with_keys):
        for part in range(parts):
            start = part * COLS
            columns = slice(start, start + COLS)
            for side in range(2):
                rows = halo[tick, side].reshape(pieces * half, features)
                first = side * (half + chunk)
                value = dot(rows, w_in[:, 2 * features + start : 2 * features + start + COLS]).astype(BF16)
                if with_keys:
                    key = head_unit(
                        dot(rows, w_in[:, features + start : features + start + COLS]), head_width
                    )
                for piece in range(pieces):
                    mine = slice(piece * half, (piece + 1) * half)
                    values[piece, first : first + half, columns] = value[mine]
                    if with_keys:
                        keys[piece, first : first + half, columns] = key[mine]

    def soften(scores, group, head, keep):
        factor = head_scale[group * per_group + head] * math.log2(math.e)
        raised = jnp.exp2(scores * factor)
        if keep is not None:
            raised = raised * keep
        return (raised * (1.0 / jnp.sum(raised, axis=-1, keepdims=True))).astype(BF16)

    def score_even(piece, group):
        columns = slice(group * LANES, (group + 1) * LANES)
        key = keys[piece, half : half + chunk, columns]
        return lax.dot_general(
            queries[piece, :, columns],
            jnp.concatenate([key * mark_row for mark_row in own], axis=0),
            (((1,), (1,)), ((), ())),
            preferred_element_type=F32,
        )

    def mix_even(piece, group, scores):
        columns = slice(group * LANES, (group + 1) * LANES)
        value = values[piece, half : half + chunk, columns]
        weights = [
            soften(scores[:, head * chunk : (head + 1) * chunk], group, head, None)
            for head in range(per_group)
        ]
        attended[piece, :, columns] = dot(
            jnp.concatenate(weights, axis=1),
            jnp.concatenate([value * mark_row for mark_row in own], axis=0),
        )

    def score_odd(piece, group):
        columns = slice(group * LANES, (group + 1) * LANES)
        query = queries[piece, :, columns]
        return lax.dot_general(
            jnp.concatenate([query * mark_row for mark_row in own], axis=0),
            keys[piece, :, columns],
            (((1,), (1,)), ((), ())),
            preferred_element_type=F32,
        )

    def mix_odd(piece, group, scores):
        columns = slice(group * LANES, (group + 1) * LANES)
        for side in range(2):
            value = values[piece, side * chunk : (side + 1) * chunk, columns]
            weights = []
            for head in range(per_group):
                first = head * chunk + side * half
                mine = scores[first : first + half, side * chunk : (side + 1) * chunk]
                weights.append(soften(mine, group, head, keeps[side]))
            attended[piece, side * half : (side + 1) * half, columns] = dot(
                jnp.concatenate(weights, axis=1),
                jnp.concatenate([value * mark_row for mark_row in own], axis=0),
            )

    def attend(some_pieces, score, mix):
        waiting = []
        for piece in some_pieces:
            for group in range(features // LANES):
                waiting.append((piece, group, score(piece, group)))
                if len(waiting) > AHEAD:
                    mix(*waiting.pop(0))
        for unit in waiting:
            mix(*unit)

    def spread(group, inner, store):
        columns = slice(group * LANES, (group + 1) * LANES)
        reach = WIN_LAT // 2
        for row in range(band_rows):
            steps = [
                step
                for step in range(WIN_LAT + 1)
                if (0 <= row + step - reach < band_rows) == inner
            ]
            sums = [None] * 3
            for step in steps:
                strip = jnp.concatenate(
                    [
                        values[piece, (row + step) * span : (row + step + 1) * span, columns]
                        for piece in range(pieces)
                    ],
                    axis=0,
                ).astype(F32)
                for lon in range(3):
                    term = position_kernel[step * 3 + lon, :, columns] * strip
                    sums[lon] = term if sums[lon] is None else sums[lon] + term
            total = sums[1] + pltpu.roll(sums[0], 1, 0) + pltpu.roll(sums[2], lon_cells - 1, 0)
            store(row, columns, total)

    def spread_own():
        for group in range(features // LANES):

            def store(row, columns, total):
                for piece in range(pieces):
                    position[piece, row * span : (row + 1) * span, columns] = total[
                        piece * span : (piece + 1) * span
                    ]

            spread(group, True, store)

    def blend(target):
        for group in range(features // LANES):

            def store(row, columns, total):
                for piece in range(pieces):
                    rows = slice(row * span, (row + 1) * span)
                    target[piece, rows, columns] = (
                        total[piece * span : (piece + 1) * span]
                        + position[piece, rows, columns]
                        + attended[piece, rows, columns]
                    ).astype(BF16)

            spread(group, False, store)

    for tick in range(TICKS):
        member = lax.rem(section - tick + section_count * TICKS, section_count)
        code = codes[tick, member]
        table_row = lax.broadcasted_iota(jnp.int32, table.shape, 0)
        perturb = jnp.sum(jnp.where(table_row == code, table[...], 0.0), axis=0, keepdims=True)
        everything = range(pieces)

        @pl.when(even)
        def _():
            for piece in everything:
                if tick:
                    with mark(f"e{tick}ring{piece}"):
                        ring_copy(tick - 1, piece).wait_recv()
                with mark(f"e{tick}enter{piece}"):
                    enter(tick, piece, perturb, normed.at[tick])
                if tick:
                    start_halo(tick, [piece])
                elif piece == 0:
                    with mark("e0load"):
                        for load in loads[small:wide]:
                            load.wait()
                with mark(f"e{tick}own{piece}"):
                    project_own(tick, piece)
                    attend([piece], score_even, mix_even)
            if tick == 0:
                with mark("e0barrier"):
                    wait_barrier()
                start_halo(tick, everything)
            with mark(f"e{tick}spread"):
                spread_own()
            with mark(f"e{tick}halowait"):
                wait_halo(tick)
            with mark(f"e{tick}after"):
                project_halo(tick, False)
                blend(blended)

        @pl.when(odd)
        def _():
            for piece in everything:
                if tick:
                    with mark(f"o{tick}ring{piece}"):
                        ring_copy(tick - 1, piece).wait_recv()
                with mark(f"o{tick}enter{piece}"):
                    enter(tick, piece, perturb, normed_here)
            with mark(f"o{tick}roll"):
                if tick == 0:
                    fill_order()

                def take(columns):
                    return normed_here[:, :, columns].reshape(tokens, COLS)

                def give(piece, columns, moved):
                    normed[tick, piece, :, columns] = moved

                roll_rows(0, take, give)
            if tick == 0:
                with mark("o0barrier"):
                    wait_barrier()
            start_halo(tick, everything)
            if tick == 0:
                with mark("o0load"):
                    for load in loads[small:wide]:
                        load.wait()
            with mark(f"o{tick}own"):
                for piece in everything:
                    project_own(tick, piece)
                spread_own()
            with mark(f"o{tick}halowait"):
                wait_halo(tick)
            with mark(f"o{tick}after"):
                project_halo(tick, True)
                attend(everything, score_odd, mix_odd)
                blend(rolled)

                def take_back(columns):
                    return rolled[:, :, columns].reshape(tokens, COLS)

                def give_back(piece, columns, moved):
                    blended[piece, :, columns] = moved

                roll_rows(1, take_back, give_back)

        drain_halo(tick)
        if tick == 0:
            with mark("load2"):
                for load in loads[wide:]:
                    load.wait()
        for piece in everything:
            with mark(f"t{tick}mlp{piece}"):
                rows = slice(piece * chunk, (piece + 1) * chunk)
                for part in range(parts):
                    columns = slice(part * COLS, (part + 1) * COLS)
                    mixed[rows, columns] = stream[rows, columns] + dot(blended[piece], w_out[:, columns])
                for first in range(piece * chunk, (piece + 1) * chunk, ROWS):
                    block = slice(first, first + ROWS)
                    normed_mix[block, :] = norm_scale(mixed[block, :], feed_gain[...]).astype(BF16)
                for start in range(0, w_up.shape[1], COLS):
                    columns = slice(start, start + COLS)
                    raw = dot(normed_mix[rows, :], w_up[:, columns])
                    hidden[rows, columns] = (raw * 0.5 * (1.0 + lax.erf(raw * math.sqrt(0.5)))).astype(BF16)
                middle = w_down.shape[0] // 2
                for part in range(parts):
                    columns = slice(part * COLS, (part + 1) * COLS)
                    finished = (
                        mixed[rows, columns]
                        + dot(hidden[rows, :middle], w_down[:middle, columns])
                        + dot(hidden[rows, middle:], w_down[middle:, columns])
                    )
                    if tick + 1 < TICKS:
                        ring_out[tick, piece, :, columns] = finished.astype(BF16)
                    else:
                        for row in range(band_rows):
                            result[row * lon_cells + piece * span : row * lon_cells + (piece + 1) * span, columns] = (
                                finished[row * span : (row + 1) * span]
                            )
            if tick + 1 < TICKS:
                ring_copy(tick, piece).start()

    for tick in range(TICKS - 1):
        for piece in range(pieces):
            ring_copy(tick, piece).wait_send()


def solution(mesh):
    section_count = mesh.shape["section"]
    band_count = mesh.shape["lat"]

    def body(
        member_slabs,
        member_codes,
        member_table,
        land_sea,
        land_embed,
        attention_gain,
        project_in,
        logit_scale,
        position_kernel,
        project_out,
        feed_gain,
        expand_weight,
        reduce_weight,
        window_offset,
    ):
        _, band_rows, lon_cells, features = member_slabs.shape
        assert band_rows == WIN_LAT
        tokens = band_rows * lon_cells
        pieces = lon_cells // WIN_LON
        chunk = tokens // pieces
        half = chunk // 2
        hidden_width = expand_weight.shape[2]
        heads = logit_scale.shape[1]
        head_width = features // heads
        links = max(TICKS - 1, 1)
        taps = position_kernel.reshape(-1, 1, features)
        operands = (
            member_codes,
            window_offset.reshape(1, 1),
            logit_scale[0],
            member_slabs[0],
            member_table,
            land_sea,
            land_embed,
            attention_gain,
            feed_gain,
            taps,
            project_in[0],
            project_out[0],
            expand_weight[0],
            reduce_weight[0],
        )
        updated = pl.pallas_call(
            functools.partial(kernel, (section_count, band_count, head_width)),
            out_shape=pltpu.VMEM((tokens, features), F32),
            in_specs=[pl.BlockSpec(memory_space=pltpu.HBM)] * len(operands),
            out_specs=pl.BlockSpec(memory_space=pltpu.VMEM),
            scratch_shapes=[
                pltpu.SMEM(member_codes.shape, jnp.int32),
                pltpu.SMEM((1, 1), jnp.int32),
                pltpu.SMEM((heads,), F32),
                pltpu.VMEM((pieces, band_rows, WIN_LON, features), F32),
                pltpu.VMEM(member_table.shape, F32),
                pltpu.VMEM(land_sea.shape, jnp.int32),
                pltpu.VMEM(land_embed.shape, F32),
                pltpu.VMEM(attention_gain.shape, F32),
                pltpu.VMEM(feed_gain.shape, F32),
                pltpu.VMEM(taps.shape, F32),
                pltpu.VMEM((features, 3 * features), BF16),
                pltpu.VMEM((features, features), BF16),
                pltpu.VMEM((features, hidden_width), BF16),
                pltpu.VMEM((hidden_width, features), BF16),
                pltpu.VMEM((tokens, features), F32),
                pltpu.VMEM((tokens, features), F32),
                pltpu.VMEM((pieces, chunk, features), BF16),
                pltpu.VMEM((TICKS, pieces, chunk, features), BF16),
                pltpu.VMEM((TICKS, 2, pieces, half, features), BF16),
                pltpu.VMEM((pieces, chunk, features), BF16),
                pltpu.VMEM((pieces, 2 * chunk, features), BF16),
                pltpu.VMEM((pieces, 2 * chunk, features), BF16),
                pltpu.VMEM((pieces, chunk, features), F32),
                pltpu.VMEM((pieces, chunk, features), F32),
                pltpu.VMEM((pieces, chunk, features), BF16),
                pltpu.VMEM((pieces, chunk, features), BF16),
                pltpu.VMEM((tokens, features), BF16),
                pltpu.VMEM((tokens, hidden_width), BF16),
                pltpu.VMEM((2, tokens, tokens), BF16),
                pltpu.VMEM((tokens, 1), F32),
                pltpu.VMEM((links, pieces, chunk, features), BF16),
                pltpu.VMEM((links, pieces, chunk, features), BF16),
                pltpu.SemaphoreType.DMA((pieces + 12 + 3 * (features // COLS),)),
                pltpu.SemaphoreType.DMA((TICKS, pieces, 2)),
                pltpu.SemaphoreType.DMA((TICKS, pieces, 2)),
                pltpu.SemaphoreType.DMA((links, pieces)),
                pltpu.SemaphoreType.DMA((links, pieces)),
            ],
            compiler_params=pltpu.CompilerParams(
                collective_id=0, has_side_effects=True, vmem_limit_bytes=40 * 1024 * 1024
            ),
        )(
            *[
                operand if operand.size == 1 else pltpu.with_memory_space_constraint(operand, pltpu.HBM)
                for operand in operands
            ]
        )
        return updated.reshape(member_slabs.shape)

    placed = (
        P(("groups", "section"), "lat", None, None),
        P(None, "groups"),
        P(),
        P("lat", None),
        P("section", None),
        P("section", None),
        P("section", None, None),
        P("section", None),
        P("section", None, None, None),
        P("section", None, None),
        P("section", None),
        P("section", None, None),
        P("section", None, None),
        P("section"),
    )
    return jax.shard_map(
        body,
        mesh=mesh,
        in_specs=placed,
        out_specs=P(("groups", "section"), "lat", None, None),
        check_vma=False,
    )
```

```python
import contextlib
import functools
import math

import jax
import jax.numpy as jnp
from jax import lax
from jax.experimental import pallas as pl
from jax.experimental.pallas import tpu as pltpu
from jax.sharding import PartitionSpec as P

WIN_LAT = 4
WIN_LON = 32
TICKS = 2
EPSILON = 1e-06

F32 = jnp.float32
BF16 = jnp.bfloat16
LANES = 128
COLS = 256
ROWS = 32
AHEAD = 2
MESH = pl.DeviceIdType.MESH


def mark(name):
    return contextlib.nullcontext()


def norm_scale(values, gain_row):
    mean_square = jnp.mean(values * values, axis=-1, keepdims=True)
    return values * lax.rsqrt(mean_square + EPSILON) * gain_row


def dot(left, right):
    return jnp.dot(left, right, preferred_element_type=F32)


def head_unit(values, head_width):
    groups = []
    for start in range(0, values.shape[1], LANES):
        part = values[:, start : start + LANES]
        lane = lax.broadcasted_iota(jnp.int32, part.shape, 1)
        square = part * part
        factor = None
        for low in range(0, LANES, head_width):
            inside = (lane >= low) & (lane < low + head_width)
            total = jnp.sum(jnp.where(inside, square, 0.0), axis=-1, keepdims=True)
            scale = lax.rsqrt(total + EPSILON)
            factor = scale if factor is None else jnp.where(inside, scale, factor)
        groups.append((part * factor).astype(BF16))
    return jnp.concatenate(groups, axis=1)


def kernel(
    sizes,
    codes_hbm,
    offsets_hbm,
    scale_hbm,
    slab_hbm,
    table_hbm,
    land_hbm,
    embed_hbm,
    attention_gain_hbm,
    feed_gain_hbm,
    taps_hbm,
    in_hbm,
    out_hbm,
    up_hbm,
    down_hbm,
    result,
    codes,
    offsets,
    head_scale,
    slab,
    table,
    land,
    land_embed,
    attention_gain,
    feed_gain,
    position_kernel,
    w_in,
    w_out,
    w_up,
    w_down,
    stream,
    mixed,
    normed_here,
    normed,
    halo,
    queries,
    keys,
    values,
    attended,
    position,
    rolled,
    blended,
    normed_mix,
    hidden,
    partial,
    order,
    land_column,
    ring_out,
    ring_in,
    load_sem,
    halo_send,
    halo_recv,
    ring_send,
    ring_recv,
):
    section_count, band_count, head_width = sizes
    pieces, band_rows, span, features = slab.shape
    lon_cells = pieces * span
    chunk = band_rows * span
    half = chunk // 2
    tokens = pieces * chunk
    per_group = LANES // head_width
    parts = features // COLS
    section = lax.axis_index("section")
    band = lax.axis_index("lat")
    following = lax.rem(section + 1, section_count)
    preceding = lax.rem(section + section_count - 1, section_count)
    has_low = band > 0
    has_high = band < band_count - 1
    shifted = lax.rem(section, 2)
    odd = shifted == 1
    even = shifted == 0

    barrier = pltpu.get_barrier_semaphore()
    pl.semaphore_signal(barrier, inc=1, device_id={"section": following}, device_id_type=MESH)
    pl.semaphore_signal(barrier, inc=1, device_id={"section": preceding}, device_id_type=MESH)

    @pl.when(has_low)
    def _():
        pl.semaphore_signal(barrier, inc=1, device_id={"lat": band - 1}, device_id_type=MESH)

    @pl.when(has_high)
    def _():
        pl.semaphore_signal(barrier, inc=1, device_id={"lat": band + 1}, device_id_type=MESH)

    pairs = [
        (slab_hbm.at[:, pl.ds(piece * span, span), :], slab.at[piece]) for piece in range(pieces)
    ]
    pairs += [
        (codes_hbm, codes),
        (offsets_hbm, offsets),
        (scale_hbm, head_scale),
        (table_hbm, table),
        (land_hbm, land),
        (embed_hbm, land_embed),
        (attention_gain_hbm, attention_gain),
        (feed_gain_hbm, feed_gain),
        (taps_hbm, position_kernel),
    ]
    small = len(pairs)
    pairs.append((in_hbm, w_in))
    wide = len(pairs)
    pairs += [(out_hbm, w_out), (up_hbm, w_up), (down_hbm, w_down)]
    loads = [
        pltpu.make_async_copy(source, target, load_sem.at[index])
        for index, (source, target) in enumerate(pairs)
    ]
    for load in loads:
        load.start()

    @pl.when(jnp.logical_not(has_low))
    def _():
        halo[:, :, 0] = jnp.zeros(halo.shape[:2] + halo.shape[3:], BF16)

    @pl.when(jnp.logical_not(has_high))
    def _():
        halo[:, :, 1] = jnp.zeros(halo.shape[:2] + halo.shape[3:], BF16)

    def settle():
        with mark("small"):
            for load in loads[:small]:
                load.wait()

        square = (lon_cells, lon_cells)
        diagonal = lax.broadcasted_iota(jnp.int32, square, 0) == lax.broadcasted_iota(jnp.int32, square, 1)
        for row in range(band_rows):
            marks = jnp.broadcast_to(land[row : row + 1, :].astype(F32), square)
            column = jnp.sum(jnp.where(diagonal, marks, 0.0), axis=-1, keepdims=True)
            for piece in range(pieces):
                first = piece * chunk + row * span
                land_column[first : first + span, :] = column[piece * span : (piece + 1) * span]

    def fill_order():
        offset = offsets[0, 0]
        for way, turn in enumerate((offset, lon_cells - offset)):
            for piece in range(pieces):
                for row in range(band_rows):
                    lon = lax.broadcasted_iota(jnp.int32, (span, tokens), 0) + piece * span + turn
                    lon = jnp.where(lon >= lon_cells, lon - lon_cells, lon)
                    target = lon + row * span
                    for step in range(1, pieces):
                        target = target + jnp.where(lon >= step * span, chunk - span, 0)
                    source = lax.broadcasted_iota(jnp.int32, (span, tokens), 1)
                    first = piece * chunk + row * span
                    order[way, first : first + span, :] = jnp.where(target == source, 1.0, 0.0).astype(BF16)

    lane = lax.broadcasted_iota(jnp.int32, (1, LANES), 1)
    own = [
        jnp.where((lane >= low) & (lane < low + head_width), 1.0, 0.0).astype(BF16)
        for low in range(0, LANES, head_width)
    ]
    key_lane = lax.broadcasted_iota(jnp.int32, (1, chunk), 1)
    keeps = [
        jnp.where((key_lane >= half) | has_low, 1.0, 0.0),
        jnp.where((key_lane < half) | has_high, 1.0, 0.0),
    ]

    def halo_up(tick, piece):
        return pltpu.make_async_remote_copy(
            src_ref=normed.at[tick, piece, pl.ds(half, half)],
            dst_ref=halo.at[tick, piece, 0],
            send_sem=halo_send.at[tick, piece, 0],
            recv_sem=halo_recv.at[tick, piece, 0],
            device_id={"lat": jnp.minimum(band + 1, band_count - 1)},
            device_id_type=MESH,
        )

    def halo_down(tick, piece):
        return pltpu.make_async_remote_copy(
            src_ref=normed.at[tick, piece, pl.ds(0, half)],
            dst_ref=halo.at[tick, piece, 1],
            send_sem=halo_send.at[tick, piece, 1],
            recv_sem=halo_recv.at[tick, piece, 1],
            device_id={"lat": jnp.maximum(band - 1, 0)},
            device_id_type=MESH,
        )

    def start_halo(tick, which):
        @pl.when(has_high)
        def _():
            for piece in which:
                halo_up(tick, piece).start()

        @pl.when(has_low)
        def _():
            for piece in which:
                halo_down(tick, piece).start()

    def wait_halo(tick, piece):
        @pl.when(has_high)
        def _():
            halo_down(tick, piece).wait_recv()

        @pl.when(has_low)
        def _():
            halo_up(tick, piece).wait_recv()

    def drain_halo(tick):
        @pl.when(has_high)
        def _():
            for piece in range(pieces):
                halo_up(tick, piece).wait_send()

        @pl.when(has_low)
        def _():
            for piece in range(pieces):
                halo_down(tick, piece).wait_send()

    def ring_copy(tick, piece):
        return pltpu.make_async_remote_copy(
            src_ref=ring_out.at[tick, piece],
            dst_ref=ring_in.at[tick, piece],
            send_sem=ring_send.at[tick, piece],
            recv_sem=ring_recv.at[tick, piece],
            device_id={"section": following},
            device_id_type=MESH,
        )

    def wait_weights():
        with mark("weights"):
            for load in loads[wide:]:
                load.wait()

    def wait_barrier():
        ends = (band == 0).astype(jnp.int32) + (band == band_count - 1).astype(jnp.int32)
        pl.semaphore_wait(barrier, 4 - ends)

    def enter(tick, piece, perturb, target):
        for row in range(band_rows):
            first = row * span
            rows = slice(piece * chunk + first, piece * chunk + first + span)
            if tick == 0:
                current = slab[piece, row]
            else:
                current = ring_in[tick - 1, piece, first : first + span, :].astype(F32)
            current = current + perturb + land_column[rows, :] * land_embed[...]
            stream[rows, :] = current
            target[piece, first : first + span, :] = norm_scale(current, attention_gain[...]).astype(BF16)

    def roll_rows(way, source, store):
        for piece in range(pieces):
            for part in range(parts):
                columns = slice(part * COLS, (part + 1) * COLS)
                moved = dot(order[way, piece * chunk : (piece + 1) * chunk, :], source(columns))
                store(piece, columns, moved.astype(BF16))

    def project_own(tick, piece):
        rows = normed[tick, piece]
        for part in range(parts):
            start = part * COLS
            columns = slice(start, start + COLS)
            queries[piece, :, columns] = head_unit(dot(rows, w_in[:, columns]), head_width)
            keys[piece, half : half + chunk, columns] = head_unit(
                dot(rows, w_in[:, features + start : features + start + COLS]), head_width
            )
            values[piece, half : half + chunk, columns] = dot(
                rows, w_in[:, 2 * features + start : 2 * features + start + COLS]
            ).astype(BF16)

    def project_halo(tick, piece, with_keys):
        rows = halo[tick, piece].reshape(2 * half, features)
        for part in range(parts):
            start = part * COLS
            columns = slice(start, start + COLS)
            value = dot(rows, w_in[:, 2 * features + start : 2 * features + start + COLS]).astype(BF16)
            if with_keys:
                key = head_unit(
                    dot(rows, w_in[:, features + start : features + start + COLS]), head_width
                )
            for side in range(2):
                mine = slice(side * half, (side + 1) * half)
                first = side * (half + chunk)
                values[piece, first : first + half, columns] = value[mine]
                if with_keys:
                    keys[piece, first : first + half, columns] = key[mine]

    def soften(scores, group, head, keep):
        factor = head_scale[group * per_group + head] * math.log2(math.e)
        raised = jnp.exp2(scores * factor)
        if keep is not None:
            raised = raised * keep
        return (raised * (1.0 / jnp.sum(raised, axis=-1, keepdims=True))).astype(BF16)

    def score_even(piece, group):
        columns = slice(group * LANES, (group + 1) * LANES)
        key = keys[piece, half : half + chunk, columns]
        return lax.dot_general(
            queries[piece, :, columns],
            jnp.concatenate([key * mark_row for mark_row in own], axis=0),
            (((1,), (1,)), ((), ())),
            preferred_element_type=F32,
        )

    def mix_even(piece, group, scores):
        columns = slice(group * LANES, (group + 1) * LANES)
        value = values[piece, half : half + chunk, columns]
        weights = [
            soften(scores[:, head * chunk : (head + 1) * chunk], group, head, None)
            for head in range(per_group)
        ]
        attended[piece, :, columns] = dot(
            jnp.concatenate(weights, axis=1),
            jnp.concatenate([value * mark_row for mark_row in own], axis=0),
        )

    def score_odd(piece, group):
        columns = slice(group * LANES, (group + 1) * LANES)
        query = queries[piece, :, columns]
        return lax.dot_general(
            jnp.concatenate([query * mark_row for mark_row in own], axis=0),
            keys[piece, :, columns],
            (((1,), (1,)), ((), ())),
            preferred_element_type=F32,
        )

    def mix_odd(piece, group, scores):
        columns = slice(group * LANES, (group + 1) * LANES)
        for side in range(2):
            value = values[piece, side * chunk : (side + 1) * chunk, columns]
            weights = []
            for head in range(per_group):
                first = head * chunk + side * half
                mine = scores[first : first + half, side * chunk : (side + 1) * chunk]
                weights.append(soften(mine, group, head, keeps[side]))
            attended[piece, side * half : (side + 1) * half, columns] = dot(
                jnp.concatenate(weights, axis=1),
                jnp.concatenate([value * mark_row for mark_row in own], axis=0),
            )

    def attend(some_pieces, score, mix):
        waiting = []
        for piece in some_pieces:
            for group in range(features // LANES):
                waiting.append((piece, group, score(piece, group)))
                if len(waiting) > AHEAD:
                    mix(*waiting.pop(0))
        for unit in waiting:
            mix(*unit)

    def spread(group, inner, store):
        columns = slice(group * LANES, (group + 1) * LANES)
        reach = WIN_LAT // 2
        for row in range(band_rows):
            steps = [
                step
                for step in range(WIN_LAT + 1)
                if (0 <= row + step - reach < band_rows) == inner
            ]
            sums = [None] * 3
            for step in steps:
                strip = jnp.concatenate(
                    [
                        values[piece, (row + step) * span : (row + step + 1) * span, columns]
                        for piece in range(pieces)
                    ],
                    axis=0,
                ).astype(F32)
                for lon in range(3):
                    term = position_kernel[step * 3 + lon, :, columns] * strip
                    sums[lon] = term if sums[lon] is None else sums[lon] + term
            total = sums[1] + pltpu.roll(sums[0], 1, 0) + pltpu.roll(sums[2], lon_cells - 1, 0)
            store(row, columns, total)

    def spread_own():
        for group in range(features // LANES):

            def store(row, columns, total):
                for piece in range(pieces):
                    position[piece, row * span : (row + 1) * span, columns] = total[
                        piece * span : (piece + 1) * span
                    ]

            spread(group, True, store)

    def blend(target):
        for group in range(features // LANES):

            def store(row, columns, total):
                for piece in range(pieces):
                    rows = slice(row * span, (row + 1) * span)
                    target[piece, rows, columns] = (
                        total[piece * span : (piece + 1) * span]
                        + position[piece, rows, columns]
                        + attended[piece, rows, columns]
                    ).astype(BF16)

            spread(group, False, store)

    def leave(some_pieces):
        for piece in some_pieces:
            rows = slice(piece * chunk, (piece + 1) * chunk)
            for part in range(parts):
                columns = slice(part * COLS, (part + 1) * COLS)
                mixed[rows, columns] = stream[rows, columns] + dot(blended[piece], w_out[:, columns])
        for piece in some_pieces:
            for first in range(piece * chunk, (piece + 1) * chunk, ROWS):
                block = slice(first, first + ROWS)
                normed_mix[block, :] = norm_scale(mixed[block, :], feed_gain[...]).astype(BF16)

    def expand(piece):
        rows = slice(piece * chunk, (piece + 1) * chunk)
        for start in range(0, w_up.shape[1], COLS):
            columns = slice(start, start + COLS)
            raw = dot(normed_mix[rows, :], w_up[:, columns])
            hidden[rows, columns] = (raw * 0.5 * (1.0 + lax.erf(raw * math.sqrt(0.5)))).astype(BF16)

    def finish(tick, at_once):
        with mark(f"t{tick}out"):
            leave(range(pieces) if at_once else [0])
        for piece in range(pieces):
            with mark(f"t{tick}mlp{piece}"):
                expand(piece)
                if not at_once and piece + 1 < pieces:
                    leave([piece + 1])
                contract(tick, piece)
            if tick + 1 < TICKS:
                ring_copy(tick, piece).start()

    def contract(tick, piece):
        rows = slice(piece * chunk, (piece + 1) * chunk)
        middle = w_down.shape[0] // 2
        for part in range(parts):
            columns = slice(part * COLS, (part + 1) * COLS)
            if part + 1 == parts and parts % 2:
                partial[...] = dot(hidden[rows, :middle], w_down[:middle, columns])
                finished = (
                    mixed[rows, columns] + dot(hidden[rows, middle:], w_down[middle:, columns])
                ) + partial[...]
            else:
                finished = mixed[rows, columns] + dot(hidden[rows, :], w_down[:, columns])
            if tick + 1 < TICKS:
                ring_out[tick, piece, :, columns] = finished.astype(BF16)
            else:
                for row in range(band_rows):
                    first = row * lon_cells + piece * span
                    result[first : first + span, columns] = finished[row * span : (row + 1) * span]

    everything = range(pieces)

    def embedding(tick):
        member = lax.rem(section - tick + section_count * TICKS, section_count)
        code = codes[tick, member]
        table_row = lax.broadcasted_iota(jnp.int32, table.shape, 0)
        return jnp.sum(jnp.where(table_row == code, table[...], 0.0), axis=0, keepdims=True)

    def wait_inputs():
        with mark("inload"):
            for load in loads[small:wide]:
                load.wait()

    def drain():
        for tick in range(TICKS):
            drain_halo(tick)
            if tick + 1 < TICKS:
                for piece in everything:
                    ring_copy(tick, piece).wait_send()

    @pl.when(odd)
    def _():
        settle()
        for tick in range(TICKS):
            perturb = embedding(tick)
            for piece in everything:
                if tick:
                    with mark(f"o{tick}ring{piece}"):
                        ring_copy(tick - 1, piece).wait_recv()
                with mark(f"o{tick}enter{piece}"):
                    enter(tick, piece, perturb, normed_here)
            with mark(f"o{tick}roll"):
                if tick == 0:
                    fill_order()

                def take(columns):
                    return normed_here[:, :, columns].reshape(tokens, COLS)

                def give(piece, columns, moved):
                    normed[tick, piece, :, columns] = moved

                roll_rows(0, take, give)
            if tick == 0:
                with mark("o0barrier"):
                    wait_barrier()
            start_halo(tick, [0])
            if tick == 0:
                wait_inputs()
            for piece in everything:
                with mark(f"o{tick}own{piece}"):
                    project_own(tick, piece)
                if piece + 1 < pieces:
                    start_halo(tick, [piece + 1])
            with mark(f"o{tick}spread"):
                spread_own()
            if tick == 0:
                wait_weights()
            for piece in everything:
                with mark(f"o{tick}halowait{piece}"):
                    wait_halo(tick, piece)
                with mark(f"o{tick}after{piece}"):
                    project_halo(tick, piece, True)
                    attend([piece], score_odd, mix_odd)
            with mark(f"o{tick}blend"):
                blend(rolled)

                def take_back(columns):
                    return rolled[:, :, columns].reshape(tokens, COLS)

                def give_back(piece, columns, moved):
                    blended[piece, :, columns] = moved

                roll_rows(1, take_back, give_back)
            finish(tick, tick + 1 == TICKS)
        drain()

    @pl.when(even)
    def _():
        settle()
        for tick in range(TICKS):
            perturb = embedding(tick)
            for piece in everything:
                if tick:
                    with mark(f"e{tick}ring{piece}"):
                        ring_copy(tick - 1, piece).wait_recv()
                with mark(f"e{tick}enter{piece}"):
                    enter(tick, piece, perturb, normed.at[tick])
                if tick and piece == pieces - 1:
                    start_halo(tick, [piece])
                if tick == 0 and piece == 0:
                    wait_inputs()
                with mark(f"e{tick}own{piece}"):
                    project_own(tick, piece)
                if tick == 0 and piece == 0:
                    with mark("e0barrier"):
                        wait_barrier()
                if tick == 0 or piece < pieces - 1:
                    start_halo(tick, [piece])
                with mark(f"e{tick}own{piece}"):
                    attend([piece], score_even, mix_even)
            with mark(f"e{tick}spread"):
                spread_own()
            if tick == 0:
                wait_weights()
            for piece in everything:
                with mark(f"e{tick}halowait{piece}"):
                    wait_halo(tick, piece)
                with mark(f"e{tick}after{piece}"):
                    project_halo(tick, piece, False)
                    if piece == pieces - 1:
                        blend(blended)
            finish(tick, True)
        drain()


def solution(mesh):
    section_count = mesh.shape["section"]
    band_count = mesh.shape["lat"]

    def body(
        member_slabs,
        member_codes,
        member_table,
        land_sea,
        land_embed,
        attention_gain,
        project_in,
        logit_scale,
        position_kernel,
        project_out,
        feed_gain,
        expand_weight,
        reduce_weight,
        window_offset,
    ):
        _, band_rows, lon_cells, features = member_slabs.shape
        assert band_rows == WIN_LAT
        tokens = band_rows * lon_cells
        pieces = lon_cells // WIN_LON
        chunk = tokens // pieces
        half = chunk // 2
        hidden_width = expand_weight.shape[2]
        heads = logit_scale.shape[1]
        head_width = features // heads
        links = max(TICKS - 1, 1)
        taps = position_kernel.reshape(-1, 1, features)
        operands = (
            member_codes,
            window_offset.reshape(1, 1),
            logit_scale[0],
            member_slabs[0],
            member_table,
            land_sea,
            land_embed,
            attention_gain,
            feed_gain,
            taps,
            project_in[0],
            project_out[0],
            expand_weight[0],
            reduce_weight[0],
        )
        updated = pl.pallas_call(
            functools.partial(kernel, (section_count, band_count, head_width)),
            out_shape=pltpu.VMEM((tokens, features), F32),
            in_specs=[pl.BlockSpec(memory_space=pltpu.HBM)] * len(operands),
            out_specs=pl.BlockSpec(memory_space=pltpu.VMEM),
            scratch_shapes=[
                pltpu.SMEM(member_codes.shape, jnp.int32),
                pltpu.SMEM((1, 1), jnp.int32),
                pltpu.SMEM((heads,), F32),
                pltpu.VMEM((pieces, band_rows, WIN_LON, features), F32),
                pltpu.VMEM(member_table.shape, F32),
                pltpu.VMEM(land_sea.shape, jnp.int32),
                pltpu.VMEM(land_embed.shape, F32),
                pltpu.VMEM(attention_gain.shape, F32),
                pltpu.VMEM(feed_gain.shape, F32),
                pltpu.VMEM(taps.shape, F32),
                pltpu.VMEM((features, 3 * features), BF16),
                pltpu.VMEM((features, features), BF16),
                pltpu.VMEM((features, hidden_width), BF16),
                pltpu.VMEM((hidden_width, features), BF16),
                pltpu.VMEM((tokens, features), F32),
                pltpu.VMEM((tokens, features), F32),
                pltpu.VMEM((pieces, chunk, features), BF16),
                pltpu.VMEM((TICKS, pieces, chunk, features), BF16),
                pltpu.VMEM((TICKS, pieces, 2, half, features), BF16),
                pltpu.VMEM((pieces, chunk, features), BF16),
                pltpu.VMEM((pieces, 2 * chunk, features), BF16),
                pltpu.VMEM((pieces, 2 * chunk, features), BF16),
                pltpu.VMEM((pieces, chunk, features), F32),
                pltpu.VMEM((pieces, chunk, features), F32),
                pltpu.VMEM((pieces, chunk, features), BF16),
                pltpu.VMEM((pieces, chunk, features), BF16),
                pltpu.VMEM((tokens, features), BF16),
                pltpu.VMEM((tokens, hidden_width), BF16),
                pltpu.VMEM((chunk, COLS), F32),
                pltpu.VMEM((2, tokens, tokens), BF16),
                pltpu.VMEM((tokens, 1), F32),
                pltpu.VMEM((links, pieces, chunk, features), BF16),
                pltpu.VMEM((links, pieces, chunk, features), BF16),
                pltpu.SemaphoreType.DMA((pieces + 13,)),
                pltpu.SemaphoreType.DMA((TICKS, pieces, 2)),
                pltpu.SemaphoreType.DMA((TICKS, pieces, 2)),
                pltpu.SemaphoreType.DMA((links, pieces)),
                pltpu.SemaphoreType.DMA((links, pieces)),
            ],
            compiler_params=pltpu.CompilerParams(
                collective_id=0, has_side_effects=True, vmem_limit_bytes=40 * 1024 * 1024
            ),
        )(
            *[
                operand if operand.size == 1 else pltpu.with_memory_space_constraint(operand, pltpu.HBM)
                for operand in operands
            ]
        )
        return updated.reshape(member_slabs.shape)

    placed = (
        P(("groups", "section"), "lat", None, None),
        P(None, "groups"),
        P(),
        P("lat", None),
        P("section", None),
        P("section", None),
        P("section", None, None),
        P("section", None),
        P("section", None, None, None),
        P("section", None, None),
        P("section", None),
        P("section", None, None),
        P("section", None, None),
        P("section"),
    )
    return jax.shard_map(
        body,
        mesh=mesh,
        in_specs=placed,
        out_specs=P(("groups", "section"), "lat", None, None),
        check_vma=False,
    )
```

```python
import contextlib
import functools
import math

import jax
import jax.numpy as jnp
from jax import lax
from jax.experimental import pallas as pl
from jax.experimental.pallas import tpu as pltpu
from jax.sharding import PartitionSpec as P

WIN_LAT = 4
WIN_LON = 32
TICKS = 2
EPSILON = 1e-06

F32 = jnp.float32
BF16 = jnp.bfloat16
LANES = 128
COLS = 256
ROWS = 32
AHEAD = 2
MESH = pl.DeviceIdType.MESH


def mark(name):
    return contextlib.nullcontext()


def norm_scale(values, gain_row):
    mean_square = jnp.mean(values * values, axis=-1, keepdims=True)
    return values * lax.rsqrt(mean_square + EPSILON) * gain_row


def dot(left, right):
    return jnp.dot(left, right, preferred_element_type=F32)


def head_unit(values, head_width):
    groups = []
    for start in range(0, values.shape[1], LANES):
        part = values[:, start : start + LANES]
        lane = lax.broadcasted_iota(jnp.int32, part.shape, 1)
        square = part * part
        factor = None
        for low in range(0, LANES, head_width):
            inside = (lane >= low) & (lane < low + head_width)
            total = jnp.sum(jnp.where(inside, square, 0.0), axis=-1, keepdims=True)
            scale = lax.rsqrt(total + EPSILON)
            factor = scale if factor is None else jnp.where(inside, scale, factor)
        groups.append((part * factor).astype(BF16))
    return jnp.concatenate(groups, axis=1)


def kernel(
    sizes,
    codes_hbm,
    offsets_hbm,
    scale_hbm,
    slab_hbm,
    table_hbm,
    land_hbm,
    embed_hbm,
    attention_gain_hbm,
    feed_gain_hbm,
    taps_hbm,
    in_hbm,
    out_hbm,
    up_hbm,
    down_hbm,
    result,
    codes,
    offsets,
    head_scale,
    slab,
    table,
    land,
    land_embed,
    attention_gain,
    feed_gain,
    position_kernel,
    w_in,
    w_out,
    w_up,
    w_down,
    stream,
    mixed,
    normed_here,
    normed,
    halo,
    queries,
    keys,
    values,
    attended,
    position,
    rolled,
    blended,
    normed_mix,
    hidden,
    partial,
    order,
    land_column,
    ring_out,
    ring_in,
    load_sem,
    halo_recv,
    ring_recv,
):
    section_count, band_count, head_width = sizes
    pieces, band_rows, span, features = slab.shape
    lon_cells = pieces * span
    chunk = band_rows * span
    half = chunk // 2
    tokens = pieces * chunk
    per_group = LANES // head_width
    parts = features // COLS
    section = lax.axis_index("section")
    band = lax.axis_index("lat")
    following = lax.rem(section + 1, section_count)
    preceding = lax.rem(section + section_count - 1, section_count)
    has_low = band > 0
    has_high = band < band_count - 1
    shifted = lax.rem(section, 2)
    odd = shifted == 1
    even = shifted == 0

    barrier = pltpu.get_barrier_semaphore()
    pl.semaphore_signal(barrier, inc=1, device_id={"section": following}, device_id_type=MESH)
    pl.semaphore_signal(barrier, inc=1, device_id={"section": preceding}, device_id_type=MESH)

    @pl.when(has_low)
    def _():
        pl.semaphore_signal(barrier, inc=1, device_id={"lat": band - 1}, device_id_type=MESH)

    @pl.when(has_high)
    def _():
        pl.semaphore_signal(barrier, inc=1, device_id={"lat": band + 1}, device_id_type=MESH)

    pairs = [
        (slab_hbm.at[:, pl.ds(piece * span, span), :], slab.at[piece]) for piece in range(pieces)
    ]
    pairs += [
        (codes_hbm, codes),
        (offsets_hbm, offsets),
        (scale_hbm, head_scale),
        (table_hbm, table),
        (land_hbm, land),
        (embed_hbm, land_embed),
        (attention_gain_hbm, attention_gain),
        (feed_gain_hbm, feed_gain),
        (taps_hbm, position_kernel),
    ]
    small = len(pairs)
    assert small >= TICKS * pieces * 2 + (TICKS - 1) * (pieces + 1)
    pairs.append((in_hbm, w_in))
    wide = len(pairs)
    pairs += [(out_hbm, w_out), (up_hbm, w_up), (down_hbm, w_down)]
    loads = [
        pltpu.make_async_copy(source, target, load_sem.at[index])
        for index, (source, target) in enumerate(pairs)
    ]
    for load in loads:
        load.start()

    @pl.when(jnp.logical_not(has_low))
    def _():
        halo[:, :, 0] = jnp.zeros(halo.shape[:2] + halo.shape[3:], BF16)

    @pl.when(jnp.logical_not(has_high))
    def _():
        halo[:, :, 1] = jnp.zeros(halo.shape[:2] + halo.shape[3:], BF16)

    def settle(with_order):
        for load in loads[pieces : pieces + 2]:
            load.wait()
        if with_order:
            fill_order()
        with mark("small"):
            for load in loads[pieces + 2 : small] + loads[:pieces]:
                load.wait()

        square = (lon_cells, lon_cells)
        diagonal = lax.broadcasted_iota(jnp.int32, square, 0) == lax.broadcasted_iota(jnp.int32, square, 1)
        for row in range(band_rows):
            marks = jnp.broadcast_to(land[row : row + 1, :].astype(F32), square)
            column = jnp.sum(jnp.where(diagonal, marks, 0.0), axis=-1, keepdims=True)
            for piece in range(pieces):
                first = piece * chunk + row * span
                land_column[first : first + span, :] = column[piece * span : (piece + 1) * span]

    def fill_order():
        offset = offsets[0, 0]
        for way, turn in enumerate((offset, lon_cells - offset)):
            for piece in range(pieces):
                for row in range(band_rows):
                    lon = lax.broadcasted_iota(jnp.int32, (span, tokens), 0) + piece * span + turn
                    lon = jnp.where(lon >= lon_cells, lon - lon_cells, lon)
                    target = lon + row * span
                    for step in range(1, pieces):
                        target = target + jnp.where(lon >= step * span, chunk - span, 0)
                    source = lax.broadcasted_iota(jnp.int32, (span, tokens), 1)
                    first = piece * chunk + row * span
                    order[way, first : first + span, :] = jnp.where(target == source, 1.0, 0.0).astype(BF16)

    lane = lax.broadcasted_iota(jnp.int32, (1, LANES), 1)
    own = [
        jnp.where((lane >= low) & (lane < low + head_width), 1.0, 0.0).astype(BF16)
        for low in range(0, LANES, head_width)
    ]
    key_lane = lax.broadcasted_iota(jnp.int32, (1, chunk), 1)
    keeps = [
        jnp.where((key_lane >= half) | has_low, 1.0, 0.0),
        jnp.where((key_lane < half) | has_high, 1.0, 0.0),
    ]

    def halo_up(tick, piece):
        return pltpu.make_async_remote_copy(
            src_ref=normed.at[tick, piece, pl.ds(half, half)],
            dst_ref=halo.at[tick, piece, 0],
            send_sem=load_sem.at[(tick * pieces + piece) * 2 + 0],
            recv_sem=halo_recv.at[tick, piece, 0],
            device_id={"lat": jnp.minimum(band + 1, band_count - 1)},
            device_id_type=MESH,
        )

    def halo_down(tick, piece):
        return pltpu.make_async_remote_copy(
            src_ref=normed.at[tick, piece, pl.ds(0, half)],
            dst_ref=halo.at[tick, piece, 1],
            send_sem=load_sem.at[(tick * pieces + piece) * 2 + 1],
            recv_sem=halo_recv.at[tick, piece, 1],
            device_id={"lat": jnp.maximum(band - 1, 0)},
            device_id_type=MESH,
        )

    def start_halo(tick, which):
        @pl.when(has_high)
        def _():
            for piece in which:
                halo_up(tick, piece).start()

        @pl.when(has_low)
        def _():
            for piece in which:
                halo_down(tick, piece).start()

    def wait_halo(tick, piece):
        @pl.when(has_high)
        def _():
            halo_down(tick, piece).wait_recv()

        @pl.when(has_low)
        def _():
            halo_up(tick, piece).wait_recv()

    def drain_halo(tick):
        @pl.when(has_high)
        def _():
            for piece in range(pieces):
                halo_up(tick, piece).wait_send()

        @pl.when(has_low)
        def _():
            for piece in range(pieces):
                halo_down(tick, piece).wait_send()

    def ring_copy(tick, piece, part, wide):
        columns = pl.ds(part * COLS, wide * COLS)
        return pltpu.make_async_remote_copy(
            src_ref=ring_out.at[tick, piece, :, columns],
            dst_ref=ring_in.at[tick, piece, :, columns],
            send_sem=load_sem.at[TICKS * pieces * 2 + tick * (pieces + 1) + piece + (part > 0) * pieces],
            recv_sem=ring_recv.at[tick, piece + (part > 0) * pieces],
            device_id={"section": following},
            device_id_type=MESH,
        )

    def ring_cuts(from_odd, piece):
        if from_odd and piece == 0:
            return [(0, parts - 1), (parts - 1, 1)]
        return [(0, parts)]

    def wait_ring(tick, piece, from_odd):
        for cut in ring_cuts(from_odd, piece):
            ring_copy(tick, piece, *cut).wait_recv()

    def wait_weights():
        with mark("weights"):
            for load in loads[wide:]:
                load.wait()

    def wait_barrier():
        ends = (band == 0).astype(jnp.int32) + (band == band_count - 1).astype(jnp.int32)
        pl.semaphore_wait(barrier, 4 - ends)

    def enter(tick, piece, perturb, target):
        for row in range(band_rows):
            first = row * span
            rows = slice(piece * chunk + first, piece * chunk + first + span)
            if tick == 0:
                current = slab[piece, row]
            else:
                current = ring_in[tick - 1, piece, first : first + span, :].astype(F32)
            current = current + perturb + land_column[rows, :] * land_embed[...]
            stream[rows, :] = current
            target[piece, first : first + span, :] = norm_scale(current, attention_gain[...]).astype(BF16)

    def roll_rows(way, source, store):
        for piece in range(pieces):
            for part in range(parts):
                columns = slice(part * COLS, (part + 1) * COLS)
                moved = dot(order[way, piece * chunk : (piece + 1) * chunk, :], source(columns))
                store(piece, columns, moved.astype(BF16))

    def project_own(tick, piece):
        rows = normed[tick, piece]
        for part in range(parts):
            start = part * COLS
            columns = slice(start, start + COLS)
            queries[piece, :, columns] = head_unit(dot(rows, w_in[:, columns]), head_width)
            keys[piece, half : half + chunk, columns] = head_unit(
                dot(rows, w_in[:, features + start : features + start + COLS]), head_width
            )
            values[piece, half : half + chunk, columns] = dot(
                rows, w_in[:, 2 * features + start : 2 * features + start + COLS]
            ).astype(BF16)

    def project_halo(tick, piece, with_keys):
        rows = halo[tick, piece].reshape(2 * half, features)
        for part in range(parts):
            start = part * COLS
            columns = slice(start, start + COLS)
            value = dot(rows, w_in[:, 2 * features + start : 2 * features + start + COLS]).astype(BF16)
            if with_keys:
                key = head_unit(
                    dot(rows, w_in[:, features + start : features + start + COLS]), head_width
                )
            for side in range(2):
                mine = slice(side * half, (side + 1) * half)
                first = side * (half + chunk)
                values[piece, first : first + half, columns] = value[mine]
                if with_keys:
                    keys[piece, first : first + half, columns] = key[mine]

    def soften(scores, group, head, keep):
        factor = head_scale[group * per_group + head] * math.log2(math.e)
        raised = jnp.exp2(scores * factor)
        if keep is not None:
            raised = raised * keep
        return (raised * (1.0 / jnp.sum(raised, axis=-1, keepdims=True))).astype(BF16)

    def score_even(piece, group):
        columns = slice(group * LANES, (group + 1) * LANES)
        key = keys[piece, half : half + chunk, columns]
        return lax.dot_general(
            queries[piece, :, columns],
            jnp.concatenate([key * mark_row for mark_row in own], axis=0),
            (((1,), (1,)), ((), ())),
            preferred_element_type=F32,
        )

    def mix_even(piece, group, scores):
        columns = slice(group * LANES, (group + 1) * LANES)
        value = values[piece, half : half + chunk, columns]
        weights = [
            soften(scores[:, head * chunk : (head + 1) * chunk], group, head, None)
            for head in range(per_group)
        ]
        attended[piece, :, columns] = dot(
            jnp.concatenate(weights, axis=1),
            jnp.concatenate([value * mark_row for mark_row in own], axis=0),
        )

    def score_odd(piece, group):
        columns = slice(group * LANES, (group + 1) * LANES)
        query = queries[piece, :, columns]
        return lax.dot_general(
            jnp.concatenate([query * mark_row for mark_row in own], axis=0),
            keys[piece, :, columns],
            (((1,), (1,)), ((), ())),
            preferred_element_type=F32,
        )

    def mix_odd(piece, group, scores):
        columns = slice(group * LANES, (group + 1) * LANES)
        for side in range(2):
            value = values[piece, side * chunk : (side + 1) * chunk, columns]
            weights = []
            for head in range(per_group):
                first = head * chunk + side * half
                mine = scores[first : first + half, side * chunk : (side + 1) * chunk]
                weights.append(soften(mine, group, head, keeps[side]))
            attended[piece, side * half : (side + 1) * half, columns] = dot(
                jnp.concatenate(weights, axis=1),
                jnp.concatenate([value * mark_row for mark_row in own], axis=0),
            )

    def attend(some_pieces, score, mix):
        waiting = []
        for piece in some_pieces:
            for group in range(features // LANES):
                waiting.append((piece, group, score(piece, group)))
                if len(waiting) > AHEAD:
                    mix(*waiting.pop(0))
        for unit in waiting:
            mix(*unit)

    def spread(group, inner, store):
        columns = slice(group * LANES, (group + 1) * LANES)
        reach = WIN_LAT // 2
        for row in range(band_rows):
            steps = [
                step
                for step in range(WIN_LAT + 1)
                if (0 <= row + step - reach < band_rows) == inner
            ]
            sums = [None] * 3
            for step in steps:
                strip = jnp.concatenate(
                    [
                        values[piece, (row + step) * span : (row + step + 1) * span, columns]
                        for piece in range(pieces)
                    ],
                    axis=0,
                ).astype(F32)
                for lon in range(3):
                    term = position_kernel[step * 3 + lon, :, columns] * strip
                    sums[lon] = term if sums[lon] is None else sums[lon] + term
            total = sums[1] + pltpu.roll(sums[0], 1, 0) + pltpu.roll(sums[2], lon_cells - 1, 0)
            store(row, columns, total)

    def spread_own():
        for group in range(features // LANES):

            def store(row, columns, total):
                for piece in range(pieces):
                    position[piece, row * span : (row + 1) * span, columns] = total[
                        piece * span : (piece + 1) * span
                    ]

            spread(group, True, store)

    def blend(target):
        for group in range(features // LANES):

            def store(row, columns, total):
                for piece in range(pieces):
                    rows = slice(row * span, (row + 1) * span)
                    target[piece, rows, columns] = (
                        total[piece * span : (piece + 1) * span]
                        + position[piece, rows, columns]
                        + attended[piece, rows, columns]
                    ).astype(BF16)

            spread(group, False, store)

    def leave(some_pieces):
        for piece in some_pieces:
            rows = slice(piece * chunk, (piece + 1) * chunk)
            for part in range(parts):
                columns = slice(part * COLS, (part + 1) * COLS)
                mixed[rows, columns] = stream[rows, columns] + dot(blended[piece], w_out[:, columns])
        for piece in some_pieces:
            for first in range(piece * chunk, (piece + 1) * chunk, ROWS):
                block = slice(first, first + ROWS)
                normed_mix[block, :] = norm_scale(mixed[block, :], feed_gain[...]).astype(BF16)

    def expand(piece):
        rows = slice(piece * chunk, (piece + 1) * chunk)
        for start in range(0, w_up.shape[1], COLS):
            columns = slice(start, start + COLS)
            raw = dot(normed_mix[rows, :], w_up[:, columns])
            hidden[rows, columns] = (raw * 0.5 * (1.0 + lax.erf(raw * math.sqrt(0.5)))).astype(BF16)

    def finish(tick, from_odd):
        last = tick + 1 == TICKS
        staged = from_odd and not last
        with mark(f"t{tick}out"):
            leave([0] if staged else range(pieces))
        for piece in range(pieces):
            with mark(f"t{tick}mlp{piece}"):
                expand(piece)
                if staged and piece + 1 < pieces:
                    leave([piece + 1])
                contract(tick, piece, ring_cuts(from_odd, piece))

    def contract(tick, piece, cuts):
        rows = slice(piece * chunk, (piece + 1) * chunk)
        middle = w_down.shape[0] // 2
        if parts % 2:
            partial[...] = dot(hidden[rows, :middle], w_down[:middle, (parts - 1) * COLS :])
        for part in range(parts):
            columns = slice(part * COLS, (part + 1) * COLS)
            if part + 1 == parts and parts % 2:
                finished = (
                    mixed[rows, columns] + dot(hidden[rows, middle:], w_down[middle:, columns])
                ) + partial[...]
            else:
                finished = mixed[rows, columns] + dot(hidden[rows, :], w_down[:, columns])
            if tick + 1 < TICKS:
                ring_out[tick, piece, :, columns] = finished.astype(BF16)
                for cut in cuts:
                    if part + 1 == sum(cut):
                        ring_copy(tick, piece, *cut).start()
            else:
                for row in range(band_rows):
                    first = row * lon_cells + piece * span
                    result[first : first + span, columns] = finished[row * span : (row + 1) * span]

    everything = range(pieces)

    def embedding(tick):
        member = lax.rem(section - tick + section_count * TICKS, section_count)
        code = codes[tick, member]
        table_row = lax.broadcasted_iota(jnp.int32, table.shape, 0)
        return jnp.sum(jnp.where(table_row == code, table[...], 0.0), axis=0, keepdims=True)

    def wait_inputs():
        with mark("inload"):
            for load in loads[small:wide]:
                load.wait()

    def drain(from_odd):
        for tick in range(TICKS):
            drain_halo(tick)
            if tick + 1 < TICKS:
                for piece in everything:
                    for cut in ring_cuts(from_odd, piece):
                        ring_copy(tick, piece, *cut).wait_send()

    @pl.when(odd)
    def _():
        settle(True)
        for tick in range(TICKS):
            perturb = embedding(tick)
            for piece in everything:
                if tick:
                    with mark(f"o{tick}ring{piece}"):
                        wait_ring(tick - 1, piece, False)
                with mark(f"o{tick}enter{piece}"):
                    enter(tick, piece, perturb, normed_here)
            with mark(f"o{tick}roll"):
                def take(columns):
                    return normed_here[:, :, columns].reshape(tokens, COLS)

                def give(piece, columns, moved):
                    normed[tick, piece, :, columns] = moved

                roll_rows(0, take, give)
            if tick == 0:
                with mark("o0barrier"):
                    wait_barrier()
            start_halo(tick, [0])
            if tick == 0:
                wait_inputs()
            for piece in everything:
                with mark(f"o{tick}own{piece}"):
                    project_own(tick, piece)
                if piece + 1 < pieces:
                    start_halo(tick, [piece + 1])
            with mark(f"o{tick}spread"):
                spread_own()
            if tick == 0:
                wait_weights()
            for piece in everything:
                with mark(f"o{tick}halowait{piece}"):
                    wait_halo(tick, piece)
                with mark(f"o{tick}after{piece}"):
                    project_halo(tick, piece, True)
                    attend([piece], score_odd, mix_odd)
            with mark(f"o{tick}blend"):
                blend(rolled)

                def take_back(columns):
                    return rolled[:, :, columns].reshape(tokens, COLS)

                def give_back(piece, columns, moved):
                    blended[piece, :, columns] = moved

                roll_rows(1, take_back, give_back)
            finish(tick, True)
        drain(True)

    @pl.when(even)
    def _():
        settle(False)
        for tick in range(TICKS):
            perturb = embedding(tick)
            for piece in everything:
                if tick:
                    with mark(f"e{tick}ring{piece}"):
                        wait_ring(tick - 1, piece, True)
                with mark(f"e{tick}enter{piece}"):
                    enter(tick, piece, perturb, normed.at[tick])
                if tick:
                    start_halo(tick, [piece])
                if tick == 0 and piece == 0:
                    wait_inputs()
                with mark(f"e{tick}own{piece}"):
                    project_own(tick, piece)
                if tick == 0 and piece == 0:
                    with mark("e0barrier"):
                        wait_barrier()
                if tick == 0:
                    start_halo(tick, [piece])
                with mark(f"e{tick}own{piece}"):
                    attend([piece], score_even, mix_even)
            with mark(f"e{tick}spread"):
                spread_own()
            if tick == 0:
                wait_weights()
            for piece in everything:
                with mark(f"e{tick}halowait{piece}"):
                    wait_halo(tick, piece)
                with mark(f"e{tick}after{piece}"):
                    project_halo(tick, piece, False)
                    if piece == pieces - 1:
                        blend(blended)
            finish(tick, False)
        drain(False)


def solution(mesh):
    section_count = mesh.shape["section"]
    assert section_count % 2 == 0
    band_count = mesh.shape["lat"]

    def body(
        member_slabs,
        member_codes,
        member_table,
        land_sea,
        land_embed,
        attention_gain,
        project_in,
        logit_scale,
        position_kernel,
        project_out,
        feed_gain,
        expand_weight,
        reduce_weight,
        window_offset,
    ):
        _, band_rows, lon_cells, features = member_slabs.shape
        assert band_rows == WIN_LAT
        tokens = band_rows * lon_cells
        pieces = lon_cells // WIN_LON
        chunk = tokens // pieces
        half = chunk // 2
        hidden_width = expand_weight.shape[2]
        heads = logit_scale.shape[1]
        head_width = features // heads
        links = max(TICKS - 1, 1)
        taps = position_kernel.reshape(-1, 1, features)
        operands = (
            member_codes,
            window_offset.reshape(1, 1),
            logit_scale[0],
            member_slabs[0],
            member_table,
            land_sea,
            land_embed,
            attention_gain,
            feed_gain,
            taps,
            project_in[0],
            project_out[0],
            expand_weight[0],
            reduce_weight[0],
        )
        updated = pl.pallas_call(
            functools.partial(kernel, (section_count, band_count, head_width)),
            out_shape=pltpu.VMEM((tokens, features), F32),
            in_specs=[pl.BlockSpec(memory_space=pltpu.HBM)] * len(operands),
            out_specs=pl.BlockSpec(memory_space=pltpu.VMEM),
            scratch_shapes=[
                pltpu.SMEM(member_codes.shape, jnp.int32),
                pltpu.SMEM((1, 1), jnp.int32),
                pltpu.SMEM((heads,), F32),
                pltpu.VMEM((pieces, band_rows, WIN_LON, features), F32),
                pltpu.VMEM(member_table.shape, F32),
                pltpu.VMEM(land_sea.shape, jnp.int32),
                pltpu.VMEM(land_embed.shape, F32),
                pltpu.VMEM(attention_gain.shape, F32),
                pltpu.VMEM(feed_gain.shape, F32),
                pltpu.VMEM(taps.shape, F32),
                pltpu.VMEM((features, 3 * features), BF16),
                pltpu.VMEM((features, features), BF16),
                pltpu.VMEM((features, hidden_width), BF16),
                pltpu.VMEM((hidden_width, features), BF16),
                pltpu.VMEM((tokens, features), F32),
                pltpu.VMEM((tokens, features), F32),
                pltpu.VMEM((pieces, chunk, features), BF16),
                pltpu.VMEM((TICKS, pieces, chunk, features), BF16),
                pltpu.VMEM((TICKS, pieces, 2, half, features), BF16),
                pltpu.VMEM((pieces, chunk, features), BF16),
                pltpu.VMEM((pieces, 2 * chunk, features), BF16),
                pltpu.VMEM((pieces, 2 * chunk, features), BF16),
                pltpu.VMEM((pieces, chunk, features), F32),
                pltpu.VMEM((pieces, chunk, features), F32),
                pltpu.VMEM((pieces, chunk, features), BF16),
                pltpu.VMEM((pieces, chunk, features), BF16),
                pltpu.VMEM((tokens, features), BF16),
                pltpu.VMEM((tokens, hidden_width), BF16),
                pltpu.VMEM((chunk, COLS), F32),
                pltpu.VMEM((2, tokens, tokens), BF16),
                pltpu.VMEM((tokens, 1), F32),
                pltpu.VMEM((links, pieces, chunk, features), BF16),
                pltpu.VMEM((links, pieces, chunk, features), BF16),
                pltpu.SemaphoreType.DMA((pieces + 13,)),
                pltpu.SemaphoreType.DMA((TICKS, pieces, 2)),
                pltpu.SemaphoreType.DMA((links, pieces + 1)),
            ],
            compiler_params=pltpu.CompilerParams(
                collective_id=0, has_side_effects=True, vmem_limit_bytes=40 * 1024 * 1024
            ),
        )(
            *[
                operand if operand.size == 1 else pltpu.with_memory_space_constraint(operand, pltpu.HBM)
                for operand in operands
            ]
        )
        return updated.reshape(member_slabs.shape)

    placed = (
        P(("groups", "section"), "lat", None, None),
        P(None, "groups"),
        P(),
        P("lat", None),
        P("section", None),
        P("section", None),
        P("section", None, None),
        P("section", None),
        P("section", None, None, None),
        P("section", None, None),
        P("section", None),
        P("section", None, None),
        P("section", None, None),
        P("section"),
    )
    return jax.shard_map(
        body,
        mesh=mesh,
        in_specs=placed,
        out_specs=P(("groups", "section"), "lat", None, None),
        check_vma=False,
    )
```

```python
import contextlib
import functools
import math

import jax
import jax.numpy as jnp
from jax import lax
from jax.experimental import pallas as pl
from jax.experimental.pallas import tpu as pltpu
from jax.sharding import PartitionSpec as P

WIN_LAT = 4
WIN_LON = 32
TICKS = 2
EPSILON = 1e-06

F32 = jnp.float32
BF16 = jnp.bfloat16
LANES = 128
COLS = 256
ROWS = 32
AHEAD = 2
MESH = pl.DeviceIdType.MESH


def mark(name):
    return contextlib.nullcontext()


def norm_scale(values, gain_row):
    mean_square = jnp.mean(values * values, axis=-1, keepdims=True)
    return values * lax.rsqrt(mean_square + EPSILON) * gain_row


def dot(left, right):
    return jnp.dot(left, right, preferred_element_type=F32)


def head_unit(values, head_width):
    groups = []
    for start in range(0, values.shape[1], LANES):
        part = values[:, start : start + LANES]
        lane = lax.broadcasted_iota(jnp.int32, part.shape, 1)
        square = part * part
        factor = None
        for low in range(0, LANES, head_width):
            inside = (lane >= low) & (lane < low + head_width)
            total = jnp.sum(jnp.where(inside, square, 0.0), axis=-1, keepdims=True)
            scale = lax.rsqrt(total + EPSILON)
            factor = scale if factor is None else jnp.where(inside, scale, factor)
        groups.append((part * factor).astype(BF16))
    return jnp.concatenate(groups, axis=1)


def kernel(
    sizes,
    codes_hbm,
    offsets_hbm,
    scale_hbm,
    slab_hbm,
    table_hbm,
    land_hbm,
    embed_hbm,
    attention_gain_hbm,
    feed_gain_hbm,
    taps_hbm,
    in_hbm,
    out_hbm,
    up_hbm,
    down_hbm,
    result,
    codes,
    offsets,
    head_scale,
    slab,
    table,
    land,
    land_embed,
    attention_gain,
    feed_gain,
    position_kernel,
    w_in,
    w_out,
    w_up,
    w_down,
    stream,
    mixed,
    normed_here,
    normed,
    halo,
    queries,
    keys,
    values,
    attended,
    position,
    rolled,
    blended,
    normed_mix,
    hidden,
    partial,
    order,
    land_column,
    ring_out,
    ring_in,
    load_sem,
    halo_recv,
    ring_recv,
):
    section_count, band_count, head_width = sizes
    pieces, band_rows, span, features = slab.shape
    lon_cells = pieces * span
    chunk = band_rows * span
    half = chunk // 2
    tokens = pieces * chunk
    per_group = LANES // head_width
    parts = features // COLS
    section = lax.axis_index("section")
    band = lax.axis_index("lat")
    following = lax.rem(section + 1, section_count)
    preceding = lax.rem(section + section_count - 1, section_count)
    has_low = band > 0
    has_high = band < band_count - 1
    shifted = lax.rem(section, 2)
    odd = shifted == 1
    even = shifted == 0

    barrier = pltpu.get_barrier_semaphore()
    pl.semaphore_signal(barrier, inc=1, device_id={"section": following}, device_id_type=MESH)
    pl.semaphore_signal(barrier, inc=1, device_id={"section": preceding}, device_id_type=MESH)

    @pl.when(has_low)
    def _():
        pl.semaphore_signal(barrier, inc=1, device_id={"lat": band - 1}, device_id_type=MESH)

    @pl.when(has_high)
    def _():
        pl.semaphore_signal(barrier, inc=1, device_id={"lat": band + 1}, device_id_type=MESH)

    pairs = [
        (slab_hbm.at[:, pl.ds(piece * span, span), :], slab.at[piece]) for piece in range(pieces)
    ]
    pairs += [
        (codes_hbm, codes),
        (offsets_hbm, offsets),
        (scale_hbm, head_scale),
        (table_hbm, table),
        (land_hbm, land),
        (embed_hbm, land_embed),
        (attention_gain_hbm, attention_gain),
        (feed_gain_hbm, feed_gain),
        (taps_hbm, position_kernel),
    ]
    small = len(pairs)
    assert small >= TICKS * pieces * 2 + (TICKS - 1) * (pieces + 1)
    pairs.append((in_hbm, w_in))
    wide = len(pairs)
    pairs += [(out_hbm, w_out), (up_hbm, w_up), (down_hbm, w_down)]
    loads = [
        pltpu.make_async_copy(source, target, load_sem.at[index])
        for index, (source, target) in enumerate(pairs)
    ]
    for load in loads:
        load.start()

    @pl.when(jnp.logical_not(has_low))
    def _():
        halo[:, :, 0] = jnp.zeros(halo.shape[:2] + halo.shape[3:], BF16)

    @pl.when(jnp.logical_not(has_high))
    def _():
        halo[:, :, 1] = jnp.zeros(halo.shape[:2] + halo.shape[3:], BF16)

    def settle(with_order):
        for load in loads[pieces : pieces + 2]:
            load.wait()
        if with_order:
            fill_order()
        with mark("small"):
            for load in loads[pieces + 2 : small] + loads[:pieces]:
                load.wait()

        square = (lon_cells, lon_cells)
        diagonal = lax.broadcasted_iota(jnp.int32, square, 0) == lax.broadcasted_iota(jnp.int32, square, 1)
        for row in range(band_rows):
            marks = jnp.broadcast_to(land[row : row + 1, :].astype(F32), square)
            column = jnp.sum(jnp.where(diagonal, marks, 0.0), axis=-1, keepdims=True)
            for piece in range(pieces):
                first = piece * chunk + row * span
                land_column[first : first + span, :] = column[piece * span : (piece + 1) * span]

    def fill_order():
        offset = offsets[0, 0]
        for way, turn in enumerate((offset, lon_cells - offset)):
            for piece in range(pieces):
                for row in range(band_rows):
                    lon = lax.broadcasted_iota(jnp.int32, (span, tokens), 0) + piece * span + turn
                    lon = jnp.where(lon >= lon_cells, lon - lon_cells, lon)
                    target = lon + row * span
                    for step in range(1, pieces):
                        target = target + jnp.where(lon >= step * span, chunk - span, 0)
                    source = lax.broadcasted_iota(jnp.int32, (span, tokens), 1)
                    first = piece * chunk + row * span
                    order[way, first : first + span, :] = jnp.where(target == source, 1.0, 0.0).astype(BF16)

    lane = lax.broadcasted_iota(jnp.int32, (1, LANES), 1)
    own = [
        jnp.where((lane >= low) & (lane < low + head_width), 1.0, 0.0).astype(BF16)
        for low in range(0, LANES, head_width)
    ]
    key_lane = lax.broadcasted_iota(jnp.int32, (1, chunk), 1)
    keeps = [
        jnp.where((key_lane >= half) | has_low, 1.0, 0.0),
        jnp.where((key_lane < half) | has_high, 1.0, 0.0),
    ]

    def halo_up(tick, piece):
        return pltpu.make_async_remote_copy(
            src_ref=normed.at[tick, piece, pl.ds(half, half)],
            dst_ref=halo.at[tick, piece, 0],
            send_sem=load_sem.at[(tick * pieces + piece) * 2 + 0],
            recv_sem=halo_recv.at[tick, piece, 0],
            device_id={"lat": jnp.minimum(band + 1, band_count - 1)},
            device_id_type=MESH,
        )

    def halo_down(tick, piece):
        return pltpu.make_async_remote_copy(
            src_ref=normed.at[tick, piece, pl.ds(0, half)],
            dst_ref=halo.at[tick, piece, 1],
            send_sem=load_sem.at[(tick * pieces + piece) * 2 + 1],
            recv_sem=halo_recv.at[tick, piece, 1],
            device_id={"lat": jnp.maximum(band - 1, 0)},
            device_id_type=MESH,
        )

    def start_halo(tick, which):
        @pl.when(has_high)
        def _():
            for piece in which:
                halo_up(tick, piece).start()

        @pl.when(has_low)
        def _():
            for piece in which:
                halo_down(tick, piece).start()

    def wait_halo(tick, piece):
        @pl.when(has_high)
        def _():
            halo_down(tick, piece).wait_recv()

        @pl.when(has_low)
        def _():
            halo_up(tick, piece).wait_recv()

    def drain_halo(tick):
        @pl.when(has_high)
        def _():
            for piece in range(pieces):
                halo_up(tick, piece).wait_send()

        @pl.when(has_low)
        def _():
            for piece in range(pieces):
                halo_down(tick, piece).wait_send()

    def ring_copy(tick, piece, part, wide):
        columns = pl.ds(part * COLS, wide * COLS)
        return pltpu.make_async_remote_copy(
            src_ref=ring_out.at[tick, piece, :, columns],
            dst_ref=ring_in.at[tick, piece, :, columns],
            send_sem=load_sem.at[TICKS * pieces * 2 + tick * (pieces + 1) + piece + (part > 0) * pieces],
            recv_sem=ring_recv.at[tick, piece + (part > 0) * pieces],
            device_id={"section": following},
            device_id_type=MESH,
        )

    def ring_cuts(from_odd, piece):
        if from_odd and piece == 0:
            return [(0, parts - 1), (parts - 1, 1)]
        return [(0, parts)]

    def wait_ring(tick, piece, from_odd):
        for cut in ring_cuts(from_odd, piece):
            ring_copy(tick, piece, *cut).wait_recv()

    def wait_weights():
        with mark("weights"):
            for load in loads[wide:]:
                load.wait()

    def wait_barrier():
        ends = (band == 0).astype(jnp.int32) + (band == band_count - 1).astype(jnp.int32)
        pl.semaphore_wait(barrier, 4 - ends)

    def enter(tick, piece, perturb, target):
        for row in range(band_rows):
            first = row * span
            rows = slice(piece * chunk + first, piece * chunk + first + span)
            if tick == 0:
                current = slab[piece, row]
            else:
                current = ring_in[tick - 1, piece, first : first + span, :].astype(F32)
            current = current + perturb + land_column[rows, :] * land_embed[...]
            stream[rows, :] = current
            target[piece, first : first + span, :] = norm_scale(current, attention_gain[...]).astype(BF16)

    def roll_rows(way, source, store, then):
        for piece in range(pieces):
            for part in range(parts):
                columns = slice(part * COLS, (part + 1) * COLS)
                moved = dot(order[way, piece * chunk : (piece + 1) * chunk, :], source(columns))
                store(piece, columns, moved.astype(BF16))
            then(piece)

    def project_own(tick, piece):
        rows = normed[tick, piece]
        for part in range(parts):
            start = part * COLS
            columns = slice(start, start + COLS)
            queries[piece, :, columns] = head_unit(dot(rows, w_in[:, columns]), head_width)
            keys[piece, half : half + chunk, columns] = head_unit(
                dot(rows, w_in[:, features + start : features + start + COLS]), head_width
            )
            values[piece, half : half + chunk, columns] = dot(
                rows, w_in[:, 2 * features + start : 2 * features + start + COLS]
            ).astype(BF16)

    def project_halo(tick, piece, with_keys):
        rows = halo[tick, piece].reshape(2 * half, features)
        for part in range(parts):
            start = part * COLS
            columns = slice(start, start + COLS)
            value = dot(rows, w_in[:, 2 * features + start : 2 * features + start + COLS]).astype(BF16)
            if with_keys:
                key = head_unit(
                    dot(rows, w_in[:, features + start : features + start + COLS]), head_width
                )
            for side in range(2):
                mine = slice(side * half, (side + 1) * half)
                first = side * (half + chunk)
                values[piece, first : first + half, columns] = value[mine]
                if with_keys:
                    keys[piece, first : first + half, columns] = key[mine]

    def soften(scores, group, head, keep):
        factor = head_scale[group * per_group + head] * math.log2(math.e)
        raised = jnp.exp2(scores * factor)
        if keep is not None:
            raised = raised * keep
        return (raised * (1.0 / jnp.sum(raised, axis=-1, keepdims=True))).astype(BF16)

    def score_even(piece, group):
        columns = slice(group * LANES, (group + 1) * LANES)
        key = keys[piece, half : half + chunk, columns]
        return lax.dot_general(
            queries[piece, :, columns],
            jnp.concatenate([key * mark_row for mark_row in own], axis=0),
            (((1,), (1,)), ((), ())),
            preferred_element_type=F32,
        )

    def mix_even(piece, group, scores):
        columns = slice(group * LANES, (group + 1) * LANES)
        value = values[piece, half : half + chunk, columns]
        weights = [
            soften(scores[:, head * chunk : (head + 1) * chunk], group, head, None)
            for head in range(per_group)
        ]
        attended[piece, :, columns] = dot(
            jnp.concatenate(weights, axis=1),
            jnp.concatenate([value * mark_row for mark_row in own], axis=0),
        )

    def score_odd(piece, group):
        columns = slice(group * LANES, (group + 1) * LANES)
        query = queries[piece, :, columns]
        return lax.dot_general(
            jnp.concatenate([query * mark_row for mark_row in own], axis=0),
            keys[piece, :, columns],
            (((1,), (1,)), ((), ())),
            preferred_element_type=F32,
        )

    def mix_odd(piece, group, scores):
        columns = slice(group * LANES, (group + 1) * LANES)
        for side in range(2):
            value = values[piece, side * chunk : (side + 1) * chunk, columns]
            weights = []
            for head in range(per_group):
                first = head * chunk + side * half
                mine = scores[first : first + half, side * chunk : (side + 1) * chunk]
                weights.append(soften(mine, group, head, keeps[side]))
            attended[piece, side * half : (side + 1) * half, columns] = dot(
                jnp.concatenate(weights, axis=1),
                jnp.concatenate([value * mark_row for mark_row in own], axis=0),
            )

    def attend(some_pieces, score, mix):
        waiting = []
        for piece in some_pieces:
            for group in range(features // LANES):
                waiting.append((piece, group, score(piece, group)))
                if len(waiting) > AHEAD:
                    mix(*waiting.pop(0))
        for unit in waiting:
            mix(*unit)

    def spread(group, inner, store):
        columns = slice(group * LANES, (group + 1) * LANES)
        reach = WIN_LAT // 2
        for row in range(band_rows):
            steps = [
                step
                for step in range(WIN_LAT + 1)
                if (0 <= row + step - reach < band_rows) == inner
            ]
            sums = [None] * 3
            for step in steps:
                strip = jnp.concatenate(
                    [
                        values[piece, (row + step) * span : (row + step + 1) * span, columns]
                        for piece in range(pieces)
                    ],
                    axis=0,
                )
                strip = strip.astype(F32) if inner else strip
                for lon in range(3):
                    term = position_kernel[step * 3 + lon, :, columns].astype(strip.dtype) * strip
                    sums[lon] = term if sums[lon] is None else sums[lon] + term
            sums = [part.astype(F32) for part in sums]
            total = sums[1] + pltpu.roll(sums[0], 1, 0) + pltpu.roll(sums[2], lon_cells - 1, 0)
            store(row, columns, total)

    def spread_own():
        for group in range(features // LANES):

            def store(row, columns, total):
                for piece in range(pieces):
                    position[piece, row * span : (row + 1) * span, columns] = total[
                        piece * span : (piece + 1) * span
                    ]

            spread(group, True, store)

    def blend(target):
        for group in range(features // LANES):

            def store(row, columns, total):
                for piece in range(pieces):
                    rows = slice(row * span, (row + 1) * span)
                    target[piece, rows, columns] = (
                        total[piece * span : (piece + 1) * span]
                        + position[piece, rows, columns]
                        + attended[piece, rows, columns]
                    ).astype(BF16)

            spread(group, False, store)

    def leave(some_pieces):
        for piece in some_pieces:
            rows = slice(piece * chunk, (piece + 1) * chunk)
            for part in range(parts):
                columns = slice(part * COLS, (part + 1) * COLS)
                mixed[rows, columns] = stream[rows, columns] + dot(blended[piece], w_out[:, columns])
        for piece in some_pieces:
            for first in range(piece * chunk, (piece + 1) * chunk, ROWS):
                block = slice(first, first + ROWS)
                normed_mix[block, :] = norm_scale(mixed[block, :], feed_gain[...]).astype(BF16)

    def expand(piece):
        rows = slice(piece * chunk, (piece + 1) * chunk)
        for start in range(0, w_up.shape[1], COLS):
            columns = slice(start, start + COLS)
            raw = dot(normed_mix[rows, :], w_up[:, columns])
            hidden[rows, columns] = (raw * 0.5 * (1.0 + lax.erf(raw * math.sqrt(0.5)))).astype(BF16)

    def finish(tick, from_odd):
        last = tick + 1 == TICKS
        staged = from_odd and not last
        with mark(f"t{tick}out"):
            leave([0] if staged else range(pieces))
        for piece in range(pieces):
            with mark(f"t{tick}mlp{piece}"):
                expand(piece)
                if staged and piece + 1 < pieces:
                    leave([piece + 1])
                contract(tick, piece, ring_cuts(from_odd, piece))

    def contract(tick, piece, cuts):
        rows = slice(piece * chunk, (piece + 1) * chunk)
        middle = w_down.shape[0] // 2
        if parts % 2:
            partial[...] = dot(hidden[rows, :middle], w_down[:middle, (parts - 1) * COLS :])
        for part in range(parts):
            columns = slice(part * COLS, (part + 1) * COLS)
            if part + 1 == parts and parts % 2:
                finished = (
                    mixed[rows, columns] + dot(hidden[rows, middle:], w_down[middle:, columns])
                ) + partial[...]
            else:
                finished = mixed[rows, columns] + dot(hidden[rows, :], w_down[:, columns])
            if tick + 1 < TICKS:
                ring_out[tick, piece, :, columns] = finished.astype(BF16)
                for cut in cuts:
                    if part + 1 == sum(cut):
                        ring_copy(tick, piece, *cut).start()
            else:
                for row in range(band_rows):
                    first = row * lon_cells + piece * span
                    result[first : first + span, columns] = finished[row * span : (row + 1) * span]

    everything = range(pieces)

    def embedding(tick):
        member = lax.rem(section - tick + section_count * TICKS, section_count)
        code = codes[tick, member]
        table_row = lax.broadcasted_iota(jnp.int32, table.shape, 0)
        return jnp.sum(jnp.where(table_row == code, table[...], 0.0), axis=0, keepdims=True)

    def wait_inputs():
        with mark("inload"):
            for load in loads[small:wide]:
                load.wait()

    def drain(from_odd):
        for tick in range(TICKS):
            drain_halo(tick)
            if tick + 1 < TICKS:
                for piece in everything:
                    for cut in ring_cuts(from_odd, piece):
                        ring_copy(tick, piece, *cut).wait_send()

    @pl.when(odd)
    def _():
        settle(True)
        for tick in range(TICKS):
            perturb = embedding(tick)
            for piece in everything:
                if tick:
                    with mark(f"o{tick}ring{piece}"):
                        wait_ring(tick - 1, piece, False)
                with mark(f"o{tick}enter{piece}"):
                    enter(tick, piece, perturb, normed_here)
            with mark(f"o{tick}roll"):
                def take(columns):
                    return normed_here[:, :, columns].reshape(tokens, COLS)

                def give(piece, columns, moved):
                    normed[tick, piece, :, columns] = moved

                def send(piece):
                    if piece == 0:
                        if tick == 0:
                            wait_barrier()
                        start_halo(tick, [piece])

                roll_rows(0, take, give, send)
            if tick == 0:
                wait_inputs()
            for piece in everything:
                with mark(f"o{tick}own{piece}"):
                    project_own(tick, piece)
                if piece + 1 < pieces:
                    start_halo(tick, [piece + 1])
            with mark(f"o{tick}spread"):
                spread_own()
            if tick == 0:
                wait_weights()
            for piece in everything:
                with mark(f"o{tick}halowait{piece}"):
                    wait_halo(tick, piece)
                with mark(f"o{tick}after{piece}"):
                    project_halo(tick, piece, True)
                    attend([piece], score_odd, mix_odd)
            with mark(f"o{tick}blend"):
                blend(rolled)

                def take_back(columns):
                    return rolled[:, :, columns].reshape(tokens, COLS)

                def give_back(piece, columns, moved):
                    blended[piece, :, columns] = moved

                roll_rows(1, take_back, give_back, lambda piece: None)
            finish(tick, True)
        drain(True)

    @pl.when(even)
    def _():
        settle(False)
        for tick in range(TICKS):
            perturb = embedding(tick)
            for piece in everything:
                if tick:
                    with mark(f"e{tick}ring{piece}"):
                        wait_ring(tick - 1, piece, True)
                with mark(f"e{tick}enter{piece}"):
                    enter(tick, piece, perturb, normed.at[tick])
                if tick:
                    start_halo(tick, [piece])
                if tick == 0 and piece == 0:
                    wait_inputs()
                with mark(f"e{tick}own{piece}"):
                    project_own(tick, piece)
                if tick == 0 and piece == 0:
                    with mark("e0barrier"):
                        wait_barrier()
                if tick == 0:
                    start_halo(tick, [piece])
                with mark(f"e{tick}own{piece}"):
                    attend([piece], score_even, mix_even)
            with mark(f"e{tick}spread"):
                spread_own()
            if tick == 0:
                wait_weights()
            for piece in everything:
                with mark(f"e{tick}halowait{piece}"):
                    wait_halo(tick, piece)
                with mark(f"e{tick}after{piece}"):
                    project_halo(tick, piece, False)
                    if piece == pieces - 1:
                        blend(blended)
            finish(tick, False)
        drain(False)


def solution(mesh):
    section_count = mesh.shape["section"]
    assert section_count % 2 == 0
    band_count = mesh.shape["lat"]

    def body(
        member_slabs,
        member_codes,
        member_table,
        land_sea,
        land_embed,
        attention_gain,
        project_in,
        logit_scale,
        position_kernel,
        project_out,
        feed_gain,
        expand_weight,
        reduce_weight,
        window_offset,
    ):
        _, band_rows, lon_cells, features = member_slabs.shape
        assert band_rows == WIN_LAT
        tokens = band_rows * lon_cells
        pieces = lon_cells // WIN_LON
        chunk = tokens // pieces
        half = chunk // 2
        hidden_width = expand_weight.shape[2]
        heads = logit_scale.shape[1]
        head_width = features // heads
        links = max(TICKS - 1, 1)
        taps = position_kernel.reshape(-1, 1, features)
        operands = (
            member_codes,
            window_offset.reshape(1, 1),
            logit_scale[0],
            member_slabs[0],
            member_table,
            land_sea,
            land_embed,
            attention_gain,
            feed_gain,
            taps,
            project_in[0],
            project_out[0],
            expand_weight[0],
            reduce_weight[0],
        )
        updated = pl.pallas_call(
            functools.partial(kernel, (section_count, band_count, head_width)),
            out_shape=pltpu.VMEM((tokens, features), F32),
            in_specs=[pl.BlockSpec(memory_space=pltpu.HBM)] * len(operands),
            out_specs=pl.BlockSpec(memory_space=pltpu.VMEM),
            scratch_shapes=[
                pltpu.SMEM(member_codes.shape, jnp.int32),
                pltpu.SMEM((1, 1), jnp.int32),
                pltpu.SMEM((heads,), F32),
                pltpu.VMEM((pieces, band_rows, WIN_LON, features), F32),
                pltpu.VMEM(member_table.shape, F32),
                pltpu.VMEM(land_sea.shape, jnp.int32),
                pltpu.VMEM(land_embed.shape, F32),
                pltpu.VMEM(attention_gain.shape, F32),
                pltpu.VMEM(feed_gain.shape, F32),
                pltpu.VMEM(taps.shape, F32),
                pltpu.VMEM((features, 3 * features), BF16),
                pltpu.VMEM((features, features), BF16),
                pltpu.VMEM((features, hidden_width), BF16),
                pltpu.VMEM((hidden_width, features), BF16),
                pltpu.VMEM((tokens, features), F32),
                pltpu.VMEM((tokens, features), F32),
                pltpu.VMEM((pieces, chunk, features), BF16),
                pltpu.VMEM((TICKS, pieces, chunk, features), BF16),
                pltpu.VMEM((TICKS, pieces, 2, half, features), BF16),
                pltpu.VMEM((pieces, chunk, features), BF16),
                pltpu.VMEM((pieces, 2 * chunk, features), BF16),
                pltpu.VMEM((pieces, 2 * chunk, features), BF16),
                pltpu.VMEM((pieces, chunk, features), F32),
                pltpu.VMEM((pieces, chunk, features), F32),
                pltpu.VMEM((pieces, chunk, features), BF16),
                pltpu.VMEM((pieces, chunk, features), BF16),
                pltpu.VMEM((tokens, features), BF16),
                pltpu.VMEM((tokens, hidden_width), BF16),
                pltpu.VMEM((chunk, COLS), F32),
                pltpu.VMEM((2, tokens, tokens), BF16),
                pltpu.VMEM((tokens, 1), F32),
                pltpu.VMEM((links, pieces, chunk, features), BF16),
                pltpu.VMEM((links, pieces, chunk, features), BF16),
                pltpu.SemaphoreType.DMA((pieces + 13,)),
                pltpu.SemaphoreType.DMA((TICKS, pieces, 2)),
                pltpu.SemaphoreType.DMA((links, pieces + 1)),
            ],
            compiler_params=pltpu.CompilerParams(
                collective_id=0, has_side_effects=True, vmem_limit_bytes=40 * 1024 * 1024
            ),
        )(
            *[
                operand if operand.size == 1 else pltpu.with_memory_space_constraint(operand, pltpu.HBM)
                for operand in operands
            ]
        )
        return updated.reshape(member_slabs.shape)

    placed = (
        P(("groups", "section"), "lat", None, None),
        P(None, "groups"),
        P(),
        P("lat", None),
        P("section", None),
        P("section", None),
        P("section", None, None),
        P("section", None),
        P("section", None, None, None),
        P("section", None, None),
        P("section", None),
        P("section", None, None),
        P("section", None, None),
        P("section"),
    )
    return jax.shard_map(
        body,
        mesh=mesh,
        in_specs=placed,
        out_specs=P(("groups", "section"), "lat", None, None),
        check_vma=False,
    )
```
